256 devices in a mesh: bucket: 64 (over x, y, z_hi), span: 4 (over z_lo, core).
Axes of the slice: x: 4, y: 4, z: 8 (z_hi: 4, z_lo: 2; z = z_hi * 2 + z_lo), core: 2. Of those that a mesh axis runs over, the one named last changes fastest.
Arguments:
- source_table: float32 [65536, 400], P('bucket'), may hold values from -6 to 6
- target_table: float32 [65536, 400], P('bucket'), may hold values from -6 to 6
- source_state: float32 [65536], P('bucket'), may hold values from 0.001 to 0.03
- target_state: float32 [65536], P('bucket'), may hold values from 0.001 to 0.03
- relation: float32 [16, 400], replicated, may hold values from -3 to 3
- relation_state: float32 [16], replicated, may hold values from 10 to 1000
- plan: int32 [64], replicated, may hold values from 0 to 63, each once
- source_index: int32 [64, 10240], P('bucket', 'span'), may hold values from 0 to 1023
- target_index: int32 [64, 10240], P('bucket', 'span'), may hold values from 0 to 1023
- relation_index: int32 [64, 10240], P('bucket', 'span'), may hold values from 0 to 15
- edge_counts: int32 [64], P('bucket'), may hold values from 1280 to 10240, as said below
Outputs:
- new_source: float32 [65536, 400], P('bucket')
- new_target: float32 [65536, 400], P('bucket')
- new_relation: float32 [16, 400], replicated
The draws below stay inside these ranges and needn't reach their ends.
Inputs may be any that keep to these rules, and one draw needn't show every extreme that they name: `plan`: each partition index appears once. `edge_counts`: one bucket has exactly 10240 live slots and another exactly 1280.
All inputs are finite; a program needn't handle non-finite values.
Results may differ from the reference program's by a relative error of at most 0.0028.
The reference program's roundings to bfloat16 on the way count: a program that leaves them out, or rounds other values in their place, can miss the bound.
Values may be sent and summed in bfloat16 or wider, within the bound.
A program may use at most 64 MiB of HBM per device.

```python
import math
import jax
import jax.numpy as jnp
import numpy as np
from jax import lax

D = 400
ROWS = 1024
E_CH = 640
REL = 16
BUCKETS = 64
EDGES_B = 10240
TABLE = 65536


def scaled_field(key, table_rows, feature_width):
    key_col, key_row, key_base = jax.random.split(key, 3)
    column_scale = jnp.exp(jax.random.uniform(key_col, (1, feature_width), jnp.float32, -1.15, 1.15))
    row_scale = jnp.exp(jax.random.uniform(key_row, (table_rows, 1), jnp.float32, -1.15, 1.15))
    base_values = jnp.clip(jax.random.normal(key_base, (table_rows, feature_width), jnp.float32), -4.0, 4.0)
    return 0.14 * base_values * row_scale * column_scale


def draw_source_table(key, part):
    return scaled_field(jax.random.fold_in(key, 11), BUCKETS * ROWS, D)


def draw_target_table(key, part):
    return scaled_field(jax.random.fold_in(key, 12), BUCKETS * ROWS, D)


def draw_edge_counts(key, part):
    key_counts, key_first, key_second = jax.random.split(jax.random.fold_in(key, 13), 3)
    counts = jax.random.randint(key_counts, (BUCKETS,), EDGES_B // 8, EDGES_B + 1)
    first_bucket = jax.random.randint(key_first, (), 0, BUCKETS)
    second_bucket = (first_bucket + jax.random.randint(key_second, (), 1, BUCKETS)) % BUCKETS
    counts = counts.at[first_bucket].set(EDGES_B).at[second_bucket].set(EDGES_B // 8)
    return counts.astype(jnp.int32)


def with_ends(array, stream_key, least, high):
    longest = array.shape.index(max(array.shape))
    spots = []
    for shift in (0, 1):
        where = [jax.random.randint(jax.random.fold_in(stream_key, axis), (), 0, length) for axis, length in enumerate(array.shape)]
        where[longest] = (where[longest] + shift) % array.shape[longest]
        spots.append(tuple(where))
    return array.at[spots[0]].set(least).at[spots[1]].set(high)


def levels(stream_key, shape, cuts, smallest, high):
    def one(position, blocks):
        draws = jax.random.uniform(jax.random.fold_in(jax.random.fold_in(stream_key, 6), position), (blocks,), jnp.float32, smallest / len(cuts), high / len(cuts))
        return jnp.repeat(jnp.exp(draws), shape[position] // blocks).reshape((-1,) + (1,) * (len(shape) - position - 1))

    level = one(*cuts[0])
    for cut in cuts[1:]:
        level = level * one(*cut)
    return level


def rank_table(amount, slope):
    loads = [(1 << 20) // math.isqrt(standing ** slope) + 1 for standing in range(1, amount + 1)]
    deviation = 1 + sum(loads) // (1 << 30)
    return np.cumsum(np.array([max(1, weight // deviation) for weight in loads]))


def ranked(stream_key, shape, amount, slope):
    listing = rank_table(amount, slope)
    ticket = jax.random.randint(jax.random.fold_in(stream_key, 1), shape, 0, int(listing[amount - 1]))
    rank = jnp.searchsorted(jnp.asarray(listing, jnp.int32), ticket, side="right")
    return jax.random.permutation(jax.random.fold_in(stream_key, 2), amount)[rank].astype(jnp.int32)


def normal_values(stream_key, extent, spread, most, held_as=jnp.bfloat16):
    return jnp.clip(spread * jax.random.normal(stream_key, extent, jnp.float32), -most, most).astype(held_as)


def setup_inputs(seed: int = 0) -> dict:
    keys = jax.random.split(jax.random.key(seed), 12)
    return {
        "source_table": draw_source_table(jax.random.fold_in(keys[11], 71), 0),
        "target_table": draw_target_table(jax.random.fold_in(keys[11], 71), 0),
        "source_state": jnp.clip(jnp.exp(math.log(0.03) - 3.4011973 * jax.random.uniform(keys[2], (TABLE,), jnp.float32) ** levels(keys[2], (TABLE,), ((0, 64),), -0.2, 0.2)), 0.001, 0.03),
        "target_state": jnp.clip(jnp.exp(math.log(0.03) - 3.4011973 * jax.random.uniform(keys[3], (TABLE,), jnp.float32) ** levels(keys[3], (TABLE,), ((0, 64),), -0.2, 0.2)), 0.001, 0.03),
        "relation": normal_values(keys[4], (REL, D), 0.5, 3.0, jnp.float32),
        "relation_state": jnp.clip(jnp.exp(jax.random.uniform(keys[5], (REL,), jnp.float32, math.log(10.0), math.log(1000.0))), 10.0, 1000.0),
        "plan": jax.random.permutation(keys[6], BUCKETS).astype(jnp.int32),
        "source_index": with_ends(ranked(keys[7], (BUCKETS, EDGES_B), ROWS, 1), jax.random.fold_in(keys[7], 3), 0, ROWS - 1).astype(jnp.int32),
        "target_index": with_ends(ranked(keys[8], (BUCKETS, EDGES_B), ROWS, 1), jax.random.fold_in(keys[8], 3), 0, ROWS - 1).astype(jnp.int32),
        "relation_index": with_ends(ranked(keys[9], (BUCKETS, EDGES_B), REL, 2), jax.random.fold_in(keys[9], 3), 0, REL - 1).astype(jnp.int32),
        "edge_counts": draw_edge_counts(jax.random.fold_in(keys[11], 71), 0),
    }


LEARN_RATE = 0.25
NEG_WEIGHT = 0.03125

def span_terms(head_rows, relation_rows, tail_rows, live_mask):
    half_width = head_rows.shape[1] // 2
    head_float = head_rows.astype(jnp.float32)
    head_real = head_float[:, :half_width]
    head_imag = head_float[:, half_width:]
    rel_real = relation_rows[:, :half_width]
    rel_imag = relation_rows[:, half_width:]
    query_rows = jnp.concatenate([head_real * rel_real - head_imag * rel_imag, head_real * rel_imag + head_imag * rel_real], axis=1).astype(jnp.bfloat16)
    scores = lax.dot_general(query_rows, tail_rows, (((1,), (1,)), ((), ())), preferred_element_type=jnp.float32)
    diagonal = lax.broadcasted_iota(jnp.int32, scores.shape, 0) == lax.broadcasted_iota(jnp.int32, scores.shape, 1)
    weights = jnp.where(diagonal, -jax.nn.sigmoid(-scores), NEG_WEIGHT * jax.nn.sigmoid(scores))
    coefficients = (weights * live_mask[:, None] * live_mask[None, :]).astype(jnp.bfloat16)
    grad_query = jnp.dot(coefficients, tail_rows, preferred_element_type=jnp.float32)
    grad_tail = lax.dot_general(coefficients, query_rows, (((0,), (0,)), ((), ())), preferred_element_type=jnp.float32)
    query_real = grad_query[:, :half_width]
    query_imag = grad_query[:, half_width:]
    grad_head = jnp.concatenate([query_real * rel_real + query_imag * rel_imag, query_imag * rel_real - query_real * rel_imag], axis=1)
    grad_relation = jnp.concatenate([query_real * head_real + query_imag * head_imag, query_imag * head_real - query_real * head_imag], axis=1)
    return (grad_head, grad_relation, grad_tail)

def row_adagrad(weights, accumulated, gradient):
    summed = accumulated + lax.optimization_barrier(jnp.mean(gradient * gradient, axis=1))
    return weights - LEARN_RATE * gradient / jnp.sqrt(summed)[:, None]

def reference(source_table, target_table, source_state, target_state, relation, relation_state, plan, source_index, target_index, relation_index, edge_counts):
    source_low = source_table.astype(jnp.bfloat16)
    target_low = target_table.astype(jnp.bfloat16)
    span_total = EDGES_B // E_CH
    relation_iota = jnp.arange(REL, dtype=jnp.int32)

    def one_bucket(relation_grad, bucket):
        source_block = lax.dynamic_slice_in_dim(source_low, (bucket * ROWS).astype(jnp.int32), ROWS, 0)
        partner = plan[bucket]
        target_block = lax.dynamic_slice_in_dim(target_low, (partner * ROWS).astype(jnp.int32), ROWS, 0)
        live_limit = edge_counts[bucket]
        head_table = source_index[bucket].reshape(span_total, E_CH)
        tail_table = target_index[bucket].reshape(span_total, E_CH)
        kind_table = relation_index[bucket].reshape(span_total, E_CH)

        def one_span(carried, span_slot):

            def compute(values):
                source_grad, target_grad, rel_grad = values
                slots = span_slot * E_CH + jnp.arange(E_CH, dtype=jnp.int32)
                live_mask = (slots < live_limit).astype(jnp.float32)
                head_ids = lax.dynamic_index_in_dim(head_table, span_slot, 0, keepdims=False)
                tail_ids = lax.dynamic_index_in_dim(tail_table, span_slot, 0, keepdims=False)
                kind_ids = lax.dynamic_index_in_dim(kind_table, span_slot, 0, keepdims=False)
                one_hot = (kind_ids[:, None] == relation_iota[None, :]).astype(jnp.float32)
                relation_rows = jnp.dot(one_hot, relation, precision=lax.Precision.HIGHEST)
                head_rows = jnp.take(source_block, head_ids, axis=0)
                tail_rows = jnp.take(target_block, tail_ids, axis=0)
                grad_head, grad_relation, grad_tail = span_terms(head_rows, relation_rows, tail_rows, live_mask)
                rel_add = lax.dot_general(one_hot, grad_relation, (((0,), (0,)), ((), ())), precision=lax.Precision.HIGHEST)
                return (source_grad.at[head_ids].add(grad_head), target_grad.at[tail_ids].add(grad_tail), rel_grad + rel_add)

            def keep_values(values):
                return values
            result = lax.cond(span_slot * E_CH < live_limit, compute, keep_values, carried)
            return (result, None)
        start_values = (jnp.zeros((ROWS, D), jnp.float32), jnp.zeros((ROWS, D), jnp.float32), relation_grad)
        final_values, unused = lax.scan(one_span, start_values, jnp.arange(span_total, dtype=jnp.int32))
        return (final_values[2], (final_values[0], final_values[1]))
    relation_grad, grads = lax.scan(one_bucket, jnp.zeros((REL, D), jnp.float32), jnp.arange(BUCKETS, dtype=jnp.int32))
    source_grad = grads[0].reshape(BUCKETS * ROWS, D)
    inverse = jnp.zeros((BUCKETS,), jnp.int32).at[plan].set(jnp.arange(BUCKETS, dtype=jnp.int32))
    target_grad = jnp.take(grads[1], inverse, axis=0).reshape(BUCKETS * ROWS, D)
    new_source = row_adagrad(source_table, source_state, source_grad)
    new_target = row_adagrad(target_table, target_state, target_grad)
    new_relation = row_adagrad(relation, relation_state, relation_grad)
    return (new_source, new_target, new_relation)
```

```python
import functools

import jax
import jax.numpy as jnp
from jax import lax
from jax.experimental import pallas as pl
from jax.experimental.pallas import tpu as pltpu
from jax.sharding import PartitionSpec as P

MESH = pl.DeviceIdType.MESH
BF = jnp.bfloat16
F32 = jnp.float32
E_CH = 640
LEARN_RATE = 0.25
NEG_WEIGHT = 0.03125
D = 400
HALF = 200
ROWS = 1024
Q = 256
EDGES = 2560
SPANS = 4
REL = 16
TILES = 50
CH = 5
CHROWS = D // CH
CHUNK = 512


class Place:
    def __init__(self):
        self.me = lax.axis_index("bucket")
        self.s = lax.axis_index("span")
        self.x = self.me // 16
        self.y = (self.me // 4) % 4
        self.z = self.me % 4
        self.buddy = self.s + 1 - 2 * (self.s % 2)
        self.cross = (self.s + 2) % 4
        self.diag = (self.buddy + 2) % 4

    def peer(self, k):
        return ((self.x + k // 16) % 4) * 16 + ((self.y + (k // 4) % 4) % 4) * 4 + (self.z + k % 4) % 4

    def slot(self, i):
        return (61 * i + 16 * self.s) % 64

    def greet(self):
        barrier = pltpu.get_barrier_semaphore()

        def sig(k, c):
            pl.semaphore_signal(barrier, inc=1, device_id=(self.peer(k), self.s), device_id_type=MESH)
            return c

        lax.fori_loop(1, 64, sig, 0)
        for o in (self.buddy, self.cross, self.diag):
            pl.semaphore_signal(barrier, inc=1, device_id=(self.me, o), device_id_type=MESH)
        return barrier


def tile_at(ref, j, lane0=0):
    return ref.at[
        pl.ds(pl.multiple_of(16 * (j // 2), 16), 16),
        pl.ds(pl.multiple_of(lane0 + 128 * (j % 2), 128), 128),
    ]


def wait_tiles(buf, n, ssem, rsem, pc, send):
    ref = buf.at[pl.ds(0, n)]
    d = pltpu.make_async_remote_copy(
        src_ref=ref, dst_ref=ref, send_sem=ssem, recv_sem=rsem, device_id=(pc.me, pc.buddy), device_id_type=MESH
    )
    if send:
        d.wait_send()
    else:
        d.wait_recv()


def leg_one(pc, src, recv, sem_loc, ssem, rsem):
    def go(k, c):
        p = pc.peer(k)
        j = pc.slot(p)

        @pl.when(j < TILES)
        def _():
            pltpu.make_async_remote_copy(
                src_ref=tile_at(src, j), dst_ref=recv.at[pc.me], send_sem=ssem, recv_sem=rsem,
                device_id=(p, pc.s), device_id_type=MESH,
            ).start()

        return c

    mine = pc.slot(pc.me)

    @pl.when(mine < TILES)
    def _():
        pltpu.make_async_copy(tile_at(src, mine), recv.at[pc.me], sem_loc).start()

    lax.fori_loop(1, 64, go, 0)


def leg_one_wait(pc, src, recv, sem_loc, ssem, rsem):
    mine = pc.slot(pc.me)

    @pl.when(mine < TILES)
    def _():
        pltpu.make_async_copy(tile_at(src, mine), recv.at[pc.me], sem_loc).wait()
        wait_tiles(recv, 63, ssem, rsem, pc, False)


def leg_two(pc, recv, pick, send, dst, sem_loc, ssem, rsem):
    mine = pc.slot(pc.me)
    lane0 = pc.s * Q

    @pl.when(mine < TILES)
    def _():
        for i in range(64):
            send[i] = recv[pick[i]]
        pltpu.make_async_copy(send.at[pc.me], tile_at(dst, mine, lane0), sem_loc).start()

        def go(k, c):
            p = pc.peer(k)
            pltpu.make_async_remote_copy(
                src_ref=send.at[p], dst_ref=tile_at(dst, mine, lane0), send_sem=ssem, recv_sem=rsem,
                device_id=(p, pc.s), device_id_type=MESH,
            ).start()
            return c

        lax.fori_loop(1, 64, go, 0)


def leg_two_wait(pc, recv, send, dst, sem_loc, ssem, rsem):
    mine = pc.slot(pc.me)

    @pl.when(mine < TILES)
    def _():
        pltpu.make_async_copy(send.at[pc.me], tile_at(dst, mine, pc.s * Q), sem_loc).wait()
        wait_tiles(recv, TILES - 1, ssem, rsem, pc, False)

    @pl.when(mine >= TILES)
    def _():
        wait_tiles(recv, TILES, ssem, rsem, pc, False)


def legs_sent(pc, recv, s1, s2, r1):
    mine = pc.slot(pc.me)

    @pl.when(mine < TILES)
    def _():
        wait_tiles(recv, TILES - 1, s1, r1, pc, True)
        wait_tiles(recv, 63, s2, r1, pc, True)

    @pl.when(mine >= TILES)
    def _():
        wait_tiles(recv, TILES, s1, r1, pc, True)


def lanes(q, n=Q):
    return pl.ds(pl.multiple_of(q * Q, Q), n)


def gather_quarters(pc, out, ssem, rsem):
    def cp(q, c, o, i):
        ref = out.at[pl.ds(c * CHROWS, CHROWS), lanes(q)]
        return pltpu.make_async_remote_copy(
            src_ref=ref, dst_ref=ref, send_sem=ssem.at[i, c], recv_sem=rsem.at[i, c],
            device_id=(pc.me, o), device_id_type=MESH,
        )

    across = [cp(pc.s, c, pc.cross, 0) for c in range(CH)]
    beside = [cp(pc.s, c, pc.buddy, 1) for c in range(CH)]
    passed = [cp(pc.cross, c, pc.buddy, 2) for c in range(CH)]
    for c in range(CH):
        across[c].start()
        beside[c].start()
    for c in range(CH):
        across[c].wait_recv()
        passed[c].start()
    for c in range(CH):
        beside[c].wait_recv()
        passed[c].wait_recv()
    for c in range(CH):
        across[c].wait_send()
        beside[c].wait_send()
        passed[c].wait_send()


def forward_kernel(tgt, plan, out, raw, send1, recv1, send2, sem_in, sem_loc, s1, r1, s2, r2, sag, rag):
    pc = Place()
    cin = pltpu.make_async_copy(tgt.at[:, lanes(pc.s)], raw, sem_in)
    cin.start()
    barrier = pc.greet()
    cin.wait()
    send1[...] = raw[...].astype(BF)
    pl.semaphore_wait(barrier, 66)
    leg_one(pc, send1, recv1, sem_loc, s1, r1)
    leg_one_wait(pc, send1, recv1, sem_loc, s1, r1)
    leg_two(pc, recv1, plan, send2, out, sem_loc, s2, r2)
    leg_two_wait(pc, recv1, send2, out, sem_loc, s2, r2)
    gather_quarters(pc, out, sag, rag)
    legs_sent(pc, recv1, s1, s2, r1)


def forward(target_t, plan):
    dma = pltpu.SemaphoreType.DMA
    return pl.pallas_call(
        forward_kernel,
        out_shape=jax.ShapeDtypeStruct((D, ROWS), BF),
        in_specs=[pl.BlockSpec(memory_space=pl.ANY), pl.BlockSpec(memory_space=pltpu.SMEM)],
        out_specs=pl.BlockSpec(memory_space=pltpu.VMEM),
        scratch_shapes=[
            pltpu.VMEM((D, Q), F32), pltpu.VMEM((D, Q), BF),
            pltpu.VMEM((64, 16, 128), BF), pltpu.VMEM((64, 16, 128), BF),
            dma, dma, dma, dma, dma, dma, dma((3, CH)), dma((3, CH)),
        ],
        compiler_params=pltpu.CompilerParams(collective_id=0, has_side_effects=True, vmem_limit_bytes=24 << 20),
        name="forward_route",
    )(target_t, plan)


def dot(a, b, ca=1, cb=0):
    return lax.dot_general(a, b, (((ca,), (cb,)), ((), ())), preferred_element_type=F32)


def spans_kernel(src, tgt, rel, sidx, tidx, kidx, lim, plan, o_src, o_tgt, o_rel, o_inv,
                 low, heads, tails, kinds, query, head, tail, relrow, coef, gtail, ghead, grel):
    first = lax.axis_index("span") * EDGES
    for b in range(64):
        o_inv[plan[b]] = b
    low[...] = src[...].astype(BF)
    r = rel[...]
    hi = r.astype(BF)
    mid = (r - hi.astype(F32)).astype(BF)
    lo = (r - hi.astype(F32) - mid.astype(F32)).astype(BF)
    rel3 = jnp.concatenate([hi, mid, lo], axis=0)

    def gather(c, carry):
        at = pl.ds(pl.multiple_of(c * CHUNK, CHUNK), CHUNK)
        slots = first + c * CHUNK + lax.broadcasted_iota(jnp.int32, (1, CHUNK), 1)
        alive = slots < lim[0]
        rows = lax.broadcasted_iota(jnp.int32, (ROWS, CHUNK), 0)
        hot = (rows == jnp.where(alive, sidx[:, at], -1)).astype(F32).astype(BF)
        heads[:, at] = hot
        h = dot(low[...], hot)
        head[:, at] = h.astype(BF)
        kind = jnp.where(alive, kidx[:, at], -1)
        k16 = lax.broadcasted_iota(jnp.int32, (REL, CHUNK), 0)
        khot = (k16 == kind).astype(F32).astype(BF)
        kinds[:, at] = khot
        rr = dot(rel3, jnp.concatenate([khot, khot, khot], axis=0), 0, 0)
        relrow[:, at] = rr
        hr, hm, rr_, rm = h[:HALF], h[HALF:], rr[:HALF], rr[HALF:]
        query[:, at] = jnp.concatenate([hr * rr_ - hm * rm, hr * rm + hm * rr_], axis=0).astype(BF)
        hot = (rows == jnp.where(alive, tidx[:, at], -1)).astype(F32).astype(BF)
        tails[:, at] = hot
        tail[:, at] = dot(tgt[...], hot).astype(BF)
        return carry

    lax.fori_loop(0, EDGES // CHUNK, gather, 0)

    def span(k, carry):
        base = pl.multiple_of(k * E_CH, 128)
        at = pl.ds(base, E_CH)
        for b in range(E_CH // 128):
            qb = query[:, pl.ds(pl.multiple_of(base + 128 * b, 128), 128)]
            score = dot(qb, tail[:, at], 0, 0)
            for j in range(E_CH // 128):
                u = score[:, 128 * j:128 * j + 128]
                if j == b:
                    diag = lax.broadcasted_iota(jnp.int32, (128, 128), 0) == lax.broadcasted_iota(jnp.int32, (128, 128), 1)
                    w = jax.nn.sigmoid(jnp.where(diag, -u, u)) * jnp.where(diag, -1.0, NEG_WEIGHT)
                else:
                    w = jax.nn.sigmoid(u) * NEG_WEIGHT
                coef[pl.ds(128 * b, 128), pl.ds(128 * j, 128)] = w.astype(BF)
        gtail[:, at] = dot(query[:, at], coef[...]).astype(BF)
        gq = dot(tail[:, at], coef[...], 1, 1)
        gr, gm = gq[:HALF], gq[HALF:]
        rr = relrow[:, at]
        rr_, rm = rr[:HALF], rr[HALF:]
        h = head[:, at].astype(F32)
        hr, hm = h[:HALF], h[HALF:]
        ghead[:, at] = jnp.concatenate([gr * rr_ + gm * rm, gm * rr_ - gr * rm], axis=0).astype(BF)
        grel[:, at] = jnp.concatenate([gr * hr + gm * hm, gm * hr - gr * hm], axis=0).astype(BF)
        return carry

    lax.fori_loop(0, SPANS, span, 0)
    o_tgt[...] = dot(gtail[...], tails[...], 1, 1).astype(BF)
    o_src[...] = dot(ghead[...], heads[...], 1, 1).astype(BF)
    o_rel[:, 0:D] = dot(kinds[...], grel[...], 1, 1)
    o_rel[:, D:512] = jnp.zeros((REL, 512 - D), F32)


def spans(source_t, target_low, relation, sidx, tidx, kidx, counts, plan):
    vm = pl.BlockSpec(memory_space=pltpu.VMEM)
    sm = pl.BlockSpec(memory_space=pltpu.SMEM)
    return pl.pallas_call(
        spans_kernel,
        out_shape=(
            jax.ShapeDtypeStruct((D, ROWS), BF), jax.ShapeDtypeStruct((D, ROWS), BF),
            jax.ShapeDtypeStruct((REL, 512), F32), jax.ShapeDtypeStruct((64,), jnp.int32),
        ),
        in_specs=[vm, vm, vm, vm, vm, vm, sm, sm],
        out_specs=(vm, vm, vm, sm),
        scratch_shapes=[
            pltpu.VMEM((D, ROWS), BF), pltpu.VMEM((ROWS, EDGES), BF), pltpu.VMEM((ROWS, EDGES), BF), pltpu.VMEM((REL, EDGES), BF),
            pltpu.VMEM((D, EDGES), BF), pltpu.VMEM((D, EDGES), BF), pltpu.VMEM((D, EDGES), BF), pltpu.VMEM((D, EDGES), F32),
            pltpu.VMEM((E_CH, E_CH), BF), pltpu.VMEM((D, EDGES), BF), pltpu.VMEM((D, EDGES), BF), pltpu.VMEM((D, EDGES), BF),
        ],
        compiler_params=pltpu.CompilerParams(vmem_limit_bytes=50 << 20),
        name="spans",
    )(source_t, target_low, relation, sidx, tidx, kidx, counts, plan)


def back_kernel(sg, tg, rg, inv, o_src, o_tgt, o_rel,
                t1, t2send, t2, quarter, recv1, send2, half, halfin, halfx, r1buf, r2buf, r2send, rax, sem_loc, st, rt,
                s1, rc1, s2, rc2, sag, rag, srel, rrel):
    pc = Place()
    barrier = pc.greet()
    pl.semaphore_wait(barrier, 66)

    def rc(src, dst, i, o):
        return pltpu.make_async_remote_copy(
            src_ref=src, dst_ref=dst, send_sem=st.at[i], recv_sem=rt.at[i], device_id=(pc.me, o), device_id_type=MESH
        )

    def to_bucket(src, dst, i, p):
        return pltpu.make_async_remote_copy(
            src_ref=src, dst_ref=dst, send_sem=srel.at[i], recv_sem=rrel.at[i], device_id=(p, pc.s), device_id_type=MESH
        )

    ta = rc(tg.at[:, lanes(pc.diag)], t1.at[1], 0, pc.buddy)
    tb = rc(tg.at[:, lanes(pc.buddy)], t1.at[0], 1, pc.buddy)
    sa = rc(sg.at[:, lanes(pc.buddy)], halfin.at[0], 2, pc.buddy)
    sb = rc(sg.at[:, lanes(pc.diag)], halfin.at[1], 3, pc.buddy)
    ra = rc(rg, r1buf, 4, pc.buddy)
    for c in (ta, tb, ra, sa, sb):
        c.start()
    ta.wait_recv()
    t2send[...] = (tg[:, lanes(pc.cross)].astype(F32) + t1[1].astype(F32)).astype(BF)
    tc = rc(t2send, t2, 5, pc.cross)
    tc.start()
    ra.wait_recv()
    r2send[...] = rg[...] + r1buf[...]
    rb = rc(r2send, r2buf, 6, pc.cross)
    rb.start()
    sa.wait_recv()
    half[0] = (sg[:, lanes(pc.s)].astype(F32) + halfin[0].astype(F32)).astype(BF)
    sb.wait_recv()
    half[1] = (sg[:, lanes(pc.cross)].astype(F32) + halfin[1].astype(F32)).astype(BF)
    tb.wait_recv()
    tc.wait_recv()
    quarter[...] = (tg[:, lanes(pc.s)].astype(F32) + t1[0].astype(F32) + t2[...].astype(F32)).astype(BF)
    leg_one(pc, quarter, recv1, sem_loc, s1, rc1)
    rb.wait_recv()
    col = pl.ds(pl.multiple_of(pc.s * 128, 128), 128)
    px = [((pc.x + d) % 4) * 16 + pc.y * 4 + pc.z for d in (1, 2, 3)]
    py = [pc.x * 16 + ((pc.y + d) % 4) * 4 + pc.z for d in (1, 2, 3)]
    pz = [pc.x * 16 + pc.y * 4 + (pc.z + d) % 4 for d in (1, 2, 3)]

    def axis(i, coord, peers, total):
        rax[i, coord] = total
        for p in peers:
            to_bucket(rax.at[i, coord], rax.at[i, coord], i, p).start()

    def axis_wait(i, send=False):
        ref = rax.at[i, pl.ds(0, 3)]
        d = to_bucket(ref, ref, i, px[0])
        if send:
            d.wait_send()
            return None
        d.wait_recv()
        return (rax[i, 0] + rax[i, 1]) + (rax[i, 2] + rax[i, 3])

    axis(0, pc.x, px, r2send[:, col] + r2buf[:, col])
    leg_one_wait(pc, quarter, recv1, sem_loc, s1, rc1)
    leg_two(pc, recv1, inv, send2, o_tgt, sem_loc, s2, rc2)
    sc = rc(half.at[0], halfx.at[1], 7, pc.cross)
    sd = rc(half.at[1], halfx.at[0], 8, pc.cross)
    sc.start()
    sd.start()
    axis(1, pc.y, py, axis_wait(0))
    axis(2, pc.z, pz, axis_wait(1))
    sc.wait_recv()
    sd.wait_recv()
    o_src[:, lanes(pc.s)] = (half[0].astype(F32) + halfx[0].astype(F32)).astype(BF)
    o_src[:, lanes(pc.cross)] = (half[1].astype(F32) + halfx[1].astype(F32)).astype(BF)
    se = rc(o_src.at[:, lanes(pc.s)], o_src.at[:, lanes(pc.s)], 9, pc.buddy)
    sf = rc(o_src.at[:, lanes(pc.cross)], o_src.at[:, lanes(pc.cross)], 10, pc.buddy)
    se.start()
    sf.start()
    o_rel[:, col] = axis_wait(2)
    rel_out = [rc(o_rel.at[:, col], o_rel.at[:, col], 11 + i, o) for i, o in enumerate((pc.buddy, pc.cross, pc.diag))]
    for c in rel_out:
        c.start()
    leg_two_wait(pc, recv1, send2, o_tgt, sem_loc, s2, rc2)
    gather_quarters(pc, o_tgt, sag, rag)
    for c in (se, sf, *rel_out):
        c.wait_recv()
    for c in (ta, tb, tc, sa, sb, sc, sd, se, sf, ra, rb, *rel_out):
        c.wait_send()
    for i in range(3):
        axis_wait(i, True)
    legs_sent(pc, recv1, s1, s2, rc1)


def back(sg, tg, rg, inv):
    vm = pl.BlockSpec(memory_space=pltpu.VMEM)
    dma = pltpu.SemaphoreType.DMA
    two = pltpu.VMEM((2, D, Q), BF)
    one = pltpu.VMEM((D, Q), BF)
    big = pltpu.VMEM((REL, 512), F32)
    return pl.pallas_call(
        back_kernel,
        out_shape=(
            jax.ShapeDtypeStruct((D, ROWS), BF), jax.ShapeDtypeStruct((D, ROWS), BF), jax.ShapeDtypeStruct((REL, 512), F32),
        ),
        in_specs=[vm, vm, vm, pl.BlockSpec(memory_space=pltpu.SMEM)],
        out_specs=(vm, vm, vm),
        scratch_shapes=[
            two, one, one, one, pltpu.VMEM((64, 16, 128), BF), pltpu.VMEM((64, 16, 128), BF), two, two, two,
            big, big, big, pltpu.VMEM((3, 4, REL, 128), F32),
            dma, dma((14,)), dma((14,)), dma, dma, dma, dma, dma((3, CH)), dma((3, CH)), dma((3,)), dma((3,)),
        ],
        compiler_params=pltpu.CompilerParams(collective_id=1, has_side_effects=True, vmem_limit_bytes=32 << 20),
        name="back_route",
    )(sg, tg, rg, inv)


def adagrad_kernel(ws, ss, gs, wt, st, gt, wr, sr, gr, o_s, o_t, o_r):
    for w, s, g, o in ((ws, ss, gs, o_s), (wt, st, gt, o_t)):
        grad = g[...].astype(F32)
        total = s[...] + jnp.sum(grad * grad, axis=0, keepdims=True) * (1.0 / D)
        o[...] = w[...] - (LEARN_RATE * grad) / jnp.sqrt(total)

    @pl.when(pl.program_id(0) == 0)
    def _():
        grad = gr[:, 0:D]
        total = sr[...] + jnp.sum(grad * grad, axis=1, keepdims=True) * (1.0 / D)
        o_r[...] = wr[...] - (LEARN_RATE * grad) / jnp.sqrt(total)


def adagrad(ws, ss, gs, wt, st, gt, wr, sr, gr):
    n = 256
    tab = pl.BlockSpec((D, n), lambda i: (0, i))
    row = pl.BlockSpec((1, n), lambda i: (0, i))
    whole = lambda *s: pl.BlockSpec(s, lambda i: (0,) * len(s))
    return pl.pallas_call(
        adagrad_kernel,
        grid=(ROWS // n,),
        out_shape=(
            jax.ShapeDtypeStruct((D, ROWS), F32), jax.ShapeDtypeStruct((D, ROWS), F32), jax.ShapeDtypeStruct((REL, D), F32),
        ),
        in_specs=[tab, row, tab, tab, row, tab, whole(REL, D), whole(REL, 1), whole(REL, 512)],
        out_specs=(tab, tab, whole(REL, D)),
        compiler_params=pltpu.CompilerParams(vmem_limit_bytes=24 << 20),
        name="adagrad",
    )(ws, ss, gs, wt, st, gt, wr, sr, gr)


def per_device(source_table, target_table, source_state, target_state, relation, relation_state,
               plan, source_index, target_index, relation_index, edge_counts):
    source_t, target_t = source_table.T, target_table.T
    target_low = forward(target_t, plan)
    sg, tg, rg, inv = spans(source_t, target_low, relation, source_index, target_index, relation_index, edge_counts, plan)
    sg, tg, rg = back(sg, tg, rg, inv)
    ns, nt, nr = adagrad(
        source_t, source_state[None, :], sg, target_t, target_state[None, :], tg, relation, relation_state[:, None], rg
    )
    return ns.T, nt.T, nr


def solution(mesh):
    placed = (
        P("bucket", None), P("bucket", None), P("bucket"), P("bucket"), P(), P(), P(),
        P("bucket", "span"), P("bucket", "span"), P("bucket", "span"), P("bucket"),
    )
    return jax.shard_map(
        per_device,
        mesh=mesh,
        in_specs=placed,
        out_specs=(P("bucket", None), P("bucket", None), P()),
        check_vma=False,
    )
```

```python
import functools

import jax
import jax.numpy as jnp
from jax import lax
from jax.experimental import pallas as pl
from jax.experimental.pallas import tpu as pltpu
from jax.sharding import PartitionSpec as P

MESH = pl.DeviceIdType.MESH
BF = jnp.bfloat16
F32 = jnp.float32
E_CH = 640
LEARN_RATE = 0.25
NEG_WEIGHT = 0.03125
D = 400
HALF = 200
ROWS = 1024
Q = 256
EDGES = 2560
SPANS = 4
REL = 16
TILES = 50
CH = 5
CHROWS = D // CH
CHUNK = 512


class Place:
    def __init__(self):
        self.me = lax.axis_index("bucket")
        self.s = lax.axis_index("span")
        self.x = self.me // 16
        self.y = (self.me // 4) % 4
        self.z = self.me % 4
        self.buddy = self.s + 1 - 2 * (self.s % 2)
        self.cross = (self.s + 2) % 4
        self.diag = (self.buddy + 2) % 4

    def peer(self, k):
        return ((self.x + k // 16) % 4) * 16 + ((self.y + (k // 4) % 4) % 4) * 4 + (self.z + k % 4) % 4

    def slot(self, i):
        return (61 * i + 16 * self.s) % 64

    def greet(self):
        barrier = pltpu.get_barrier_semaphore()

        def sig(k, c):
            pl.semaphore_signal(barrier, inc=1, device_id=(self.peer(k), self.s), device_id_type=MESH)
            return c

        lax.fori_loop(1, 64, sig, 0)
        for o in (self.buddy, self.cross, self.diag):
            pl.semaphore_signal(barrier, inc=1, device_id=(self.me, o), device_id_type=MESH)
        return barrier


def tile_at(ref, j, lane0=0):
    return ref.at[
        pl.ds(pl.multiple_of(16 * (j // 2), 16), 16),
        pl.ds(pl.multiple_of(lane0 + 128 * (j % 2), 128), 128),
    ]


def wait_tiles(buf, n, ssem, rsem, pc, send):
    ref = buf.at[pl.ds(0, n)]
    d = pltpu.make_async_remote_copy(
        src_ref=ref, dst_ref=ref, send_sem=ssem, recv_sem=rsem, device_id=(pc.me, pc.buddy), device_id_type=MESH
    )
    if send:
        d.wait_send()
    else:
        d.wait_recv()


def leg_one(pc, src, recv, sem_loc, ssem, rsem):
    def go(k, c):
        p = pc.peer(k)
        j = pc.slot(p)

        @pl.when(j < TILES)
        def _():
            pltpu.make_async_remote_copy(
                src_ref=tile_at(src, j), dst_ref=recv.at[pc.me], send_sem=ssem, recv_sem=rsem,
                device_id=(p, pc.s), device_id_type=MESH,
            ).start()

        return c

    mine = pc.slot(pc.me)

    @pl.when(mine < TILES)
    def _():
        pltpu.make_async_copy(tile_at(src, mine), recv.at[pc.me], sem_loc).start()

    lax.fori_loop(1, 64, go, 0)


def leg_one_wait(pc, src, recv, sem_loc, ssem, rsem):
    mine = pc.slot(pc.me)

    @pl.when(mine < TILES)
    def _():
        pltpu.make_async_copy(tile_at(src, mine), recv.at[pc.me], sem_loc).wait()
        wait_tiles(recv, 63, ssem, rsem, pc, False)


def leg_two(pc, recv, pick, send, dst, sem_loc, ssem, rsem):
    mine = pc.slot(pc.me)
    lane0 = pc.s * Q

    @pl.when(mine < TILES)
    def _():
        for i in range(64):
            send[i] = recv[pick[i]]
        pltpu.make_async_copy(send.at[pc.me], tile_at(dst, mine, lane0), sem_loc).start()

        def go(k, c):
            p = pc.peer(k)
            pltpu.make_async_remote_copy(
                src_ref=send.at[p], dst_ref=tile_at(dst, mine, lane0), send_sem=ssem, recv_sem=rsem,
                device_id=(p, pc.s), device_id_type=MESH,
            ).start()
            return c

        lax.fori_loop(1, 64, go, 0)


def leg_two_wait(pc, recv, send, dst, sem_loc, ssem, rsem):
    mine = pc.slot(pc.me)

    @pl.when(mine < TILES)
    def _():
        pltpu.make_async_copy(send.at[pc.me], tile_at(dst, mine, pc.s * Q), sem_loc).wait()
        wait_tiles(recv, TILES - 1, ssem, rsem, pc, False)

    @pl.when(mine >= TILES)
    def _():
        wait_tiles(recv, TILES, ssem, rsem, pc, False)


def legs_sent(pc, recv, s1, s2, r1):
    mine = pc.slot(pc.me)

    @pl.when(mine < TILES)
    def _():
        wait_tiles(recv, TILES - 1, s1, r1, pc, True)
        wait_tiles(recv, 63, s2, r1, pc, True)

    @pl.when(mine >= TILES)
    def _():
        wait_tiles(recv, TILES, s1, r1, pc, True)


def lanes(q, n=Q):
    return pl.ds(pl.multiple_of(q * Q, Q), n)


def dot(a, b, ca=1, cb=0):
    return lax.dot_general(a, b, (((ca,), (cb,)), ((), ())), preferred_element_type=F32)


def quarter_rows(q):
    return pl.ds(pl.multiple_of(q * Q, Q), Q)


def chunk_at(c):
    return pl.ds(pl.multiple_of(c * CHUNK, CHUNK), CHUNK)


def alive_index(idx, c, first, lim):
    slots = first + c * CHUNK + lax.broadcasted_iota(jnp.int32, (1, CHUNK), 1)
    return jnp.where(slots < lim[0], idx[:, chunk_at(c)], -1)


def round_kernel(
    src, tgt, rel, sidx, tidx, kidx, lim, plan, inv,
    o_src, o_tgt, o_rel,
    raw, src_raw, low, table, heads, tails, kinds, query, head, tail, relrow, coef, gtail, ghead, grel, tg, sg,
    send1, recv1, send2, quarter, recv3, send4,
    t1, t2send, t2, half, halfin, halfx, rg, r1buf, r2buf, r2send, rax,
    sem_in, sem_loc, s1, r1, s2, r2, s3, r3, s4, r4, sag, rag, sbk, rbk, st, rt, srel, rrel,
):
    pc = Place()
    cin = pltpu.make_async_copy(tgt.at[:, lanes(pc.s)], raw, sem_in.at[0])
    cin.start()
    csrc = pltpu.make_async_copy(src, src_raw, sem_in.at[1])
    csrc.start()
    barrier = pc.greet()
    cin.wait()
    send1[...] = raw[...].astype(BF)
    pl.semaphore_wait(barrier, 66)
    leg_one(pc, send1, recv1, sem_loc.at[0], s1, r1)

    first = pc.s * EDGES
    r = rel[...]
    hi = r.astype(BF)
    mid = (r - hi.astype(F32)).astype(BF)
    lo = (r - hi.astype(F32) - mid.astype(F32)).astype(BF)
    rel3 = jnp.concatenate([hi, mid, lo], axis=0)
    csrc.wait()
    low[...] = src_raw[...].astype(BF)

    def gather_heads(c, carry):
        at = chunk_at(c)
        rows = lax.broadcasted_iota(jnp.int32, (ROWS, CHUNK), 0)
        hot = (rows == alive_index(sidx, c, first, lim)).astype(F32).astype(BF)
        heads[:, at] = hot
        h = dot(low[...], hot)
        head[:, at] = h.astype(BF)
        k16 = lax.broadcasted_iota(jnp.int32, (REL, CHUNK), 0)
        khot = (k16 == alive_index(kidx, c, first, lim)).astype(F32).astype(BF)
        kinds[:, at] = khot
        rr = dot(rel3, jnp.concatenate([khot, khot, khot], axis=0), 0, 0)
        relrow[:, at] = rr
        hr, hm, kr, km = h[:HALF], h[HALF:], rr[:HALF], rr[HALF:]
        query[:, at] = jnp.concatenate([hr * kr - hm * km, hr * km + hm * kr], axis=0).astype(BF)
        return carry

    lax.fori_loop(0, EDGES // CHUNK, gather_heads, 0)
    leg_one_wait(pc, send1, recv1, sem_loc.at[0], s1, r1)
    leg_two(pc, recv1, plan, send2, table, sem_loc.at[1], s2, r2)

    def mark_tails(c, carry):
        rows = lax.broadcasted_iota(jnp.int32, (ROWS, CHUNK), 0)
        tails[:, chunk_at(c)] = (rows == alive_index(tidx, c, first, lim)).astype(F32).astype(BF)
        return carry

    lax.fori_loop(0, EDGES // CHUNK, mark_tails, 0)
    leg_two_wait(pc, recv1, send2, table, sem_loc.at[1], s2, r2)

    def cp(out, q, c, o, i, ss, rs):
        ref = out.at[pl.ds(c * CHROWS, CHROWS), lanes(q)]
        return pltpu.make_async_remote_copy(
            src_ref=ref, dst_ref=ref, send_sem=ss.at[i, c], recv_sem=rs.at[i, c],
            device_id=(pc.me, o), device_id_type=MESH,
        )

    across = [cp(table, pc.s, c, pc.cross, 0, sag, rag) for c in range(CH)]
    beside = [cp(table, pc.s, c, pc.buddy, 1, sag, rag) for c in range(CH)]
    passed = [cp(table, pc.cross, c, pc.buddy, 2, sag, rag) for c in range(CH)]
    for c in range(CH):
        across[c].start()
        beside[c].start()
    for c in range(CH):
        beside[c].wait_recv()
    near = pl.ds(pl.multiple_of((pc.s // 2) * 512, 512), 512)
    far = pl.ds(pl.multiple_of((1 - pc.s // 2) * 512, 512), 512)

    def tails_near(c, carry):
        tail[:, chunk_at(c)] = dot(table[:, near], tails[near, chunk_at(c)]).astype(BF)
        return carry

    lax.fori_loop(0, EDGES // CHUNK, tails_near, 0)
    for c in range(CH):
        across[c].wait_recv()
        passed[c].start()
    for c in range(CH):
        passed[c].wait_recv()

    def tails_far(c, carry):
        at = chunk_at(c)
        tail[:, at] = (tail[:, at].astype(F32) + dot(table[:, far], tails[far, at])).astype(BF)
        return carry

    lax.fori_loop(0, EDGES // CHUNK, tails_far, 0)

    def score_span(k, carry):
        base = pl.multiple_of(k * E_CH, 128)
        at = pl.ds(base, E_CH)
        for b in range(E_CH // 128):
            qb = query[:, pl.ds(pl.multiple_of(base + 128 * b, 128), 128)]
            score = dot(qb, tail[:, at], 0, 0)
            for j in range(E_CH // 128):
                u = score[:, 128 * j:128 * j + 128]
                if j == b:
                    one = lax.broadcasted_iota(jnp.int32, (128, 128), 0) == lax.broadcasted_iota(jnp.int32, (128, 128), 1)
                    w = jax.nn.sigmoid(jnp.where(one, -u, u)) * jnp.where(one, -1.0, NEG_WEIGHT)
                else:
                    w = jax.nn.sigmoid(u) * NEG_WEIGHT
                coef[k, pl.ds(128 * b, 128), pl.ds(128 * j, 128)] = w.astype(BF)
        gtail[:, at] = dot(query[:, at], coef[k]).astype(BF)
        return carry

    lax.fori_loop(0, SPANS, score_span, 0)

    def rc(src_ref, dst_ref, i, o):
        return pltpu.make_async_remote_copy(
            src_ref=src_ref, dst_ref=dst_ref, send_sem=st.at[i], recv_sem=rt.at[i], device_id=(pc.me, o), device_id_type=MESH
        )

    def to_bucket(src_ref, dst_ref, i, p):
        return pltpu.make_async_remote_copy(
            src_ref=src_ref, dst_ref=dst_ref, send_sem=srel.at[i], recv_sem=rrel.at[i], device_id=(p, pc.s), device_id_type=MESH
        )

    def target_sum(q):
        tg[:, lanes(q)] = dot(gtail[...], tails[quarter_rows(q), :], 1, 1).astype(BF)

    ta = rc(tg.at[:, lanes(pc.diag)], t1.at[1], 0, pc.buddy)
    tb = rc(tg.at[:, lanes(pc.buddy)], t1.at[0], 1, pc.buddy)
    tc = rc(t2send, t2, 5, pc.cross)
    target_sum(pc.diag)
    ta.start()
    target_sum(pc.cross)
    ta.wait_recv()
    t2send[...] = (tg[:, lanes(pc.cross)].astype(F32) + t1[1].astype(F32)).astype(BF)
    tc.start()
    target_sum(pc.buddy)
    tb.start()
    target_sum(pc.s)

    def query_span(k, carry):
        at = pl.ds(pl.multiple_of(k * E_CH, 128), E_CH)
        gq = dot(tail[:, at], coef[k], 1, 1)
        gr, gm = gq[:HALF], gq[HALF:]
        rr = relrow[:, at]
        kr, km = rr[:HALF], rr[HALF:]
        h = head[:, at].astype(F32)
        hr, hm = h[:HALF], h[HALF:]
        ghead[:, at] = jnp.concatenate([gr * kr + gm * km, gm * kr - gr * km], axis=0).astype(BF)
        grel[:, at] = jnp.concatenate([gr * hr + gm * hm, gm * hr - gr * hm], axis=0).astype(BF)
        return carry

    lax.fori_loop(0, SPANS, query_span, 0)
    tb.wait_recv()
    tc.wait_recv()
    quarter[...] = (tg[:, lanes(pc.s)].astype(F32) + t1[0].astype(F32) + t2[...].astype(F32)).astype(BF)
    leg_one(pc, quarter, recv3, sem_loc.at[2], s3, r3)

    rg[:, 0:D] = dot(kinds[...], grel[...], 1, 1)
    rg[:, D:512] = jnp.zeros((REL, 512 - D), F32)
    ra = rc(rg, r1buf, 4, pc.buddy)
    ra.start()

    def source_sum(q):
        sg[:, lanes(q)] = dot(ghead[...], heads[quarter_rows(q), :], 1, 1).astype(BF)

    sa = rc(sg.at[:, lanes(pc.buddy)], halfin.at[0], 2, pc.buddy)
    sb = rc(sg.at[:, lanes(pc.diag)], halfin.at[1], 3, pc.buddy)
    source_sum(pc.buddy)
    sa.start()
    source_sum(pc.diag)
    sb.start()
    ra.wait_recv()
    r2send[...] = rg[...] + r1buf[...]
    rb = rc(r2send, r2buf, 6, pc.cross)
    rb.start()
    source_sum(pc.s)
    source_sum(pc.cross)

    leg_one_wait(pc, quarter, recv3, sem_loc.at[2], s3, r3)
    leg_two(pc, recv3, inv, send4, o_tgt, sem_loc.at[3], s4, r4)

    sc = rc(half.at[0], halfx.at[1], 7, pc.cross)
    sd = rc(half.at[1], halfx.at[0], 8, pc.cross)
    sa.wait_recv()
    half[0] = (sg[:, lanes(pc.s)].astype(F32) + halfin[0].astype(F32)).astype(BF)
    sc.start()
    sb.wait_recv()
    half[1] = (sg[:, lanes(pc.cross)].astype(F32) + halfin[1].astype(F32)).astype(BF)
    sd.start()
    rb.wait_recv()
    col = pl.ds(pl.multiple_of(pc.s * 128, 128), 128)
    px = [((pc.x + d) % 4) * 16 + pc.y * 4 + pc.z for d in (1, 2, 3)]
    py = [pc.x * 16 + ((pc.y + d) % 4) * 4 + pc.z for d in (1, 2, 3)]
    pz = [pc.x * 16 + pc.y * 4 + (pc.z + d) % 4 for d in (1, 2, 3)]

    def axis(i, coord, peers, total):
        rax[i, coord] = total
        for p in peers:
            to_bucket(rax.at[i, coord], rax.at[i, coord], i, p).start()

    def axis_wait(i, send=False):
        ref = rax.at[i, pl.ds(0, 3)]
        d = to_bucket(ref, ref, i, px[0])
        if send:
            d.wait_send()
            return None
        d.wait_recv()
        return (rax[i, 0] + rax[i, 1]) + (rax[i, 2] + rax[i, 3])

    axis(0, pc.x, px, r2send[:, col] + r2buf[:, col])
    axis(1, pc.y, py, axis_wait(0))
    axis(2, pc.z, pz, axis_wait(1))

    leg_two_wait(pc, recv3, send4, o_tgt, sem_loc.at[3], s4, r4)
    across2 = [cp(o_tgt, pc.s, c, pc.cross, 0, sbk, rbk) for c in range(CH)]
    beside2 = [cp(o_tgt, pc.s, c, pc.buddy, 1, sbk, rbk) for c in range(CH)]
    passed2 = [cp(o_tgt, pc.cross, c, pc.buddy, 2, sbk, rbk) for c in range(CH)]
    for c in range(CH):
        across2[c].start()
        beside2[c].start()

    o_rel[:, col] = axis_wait(2)
    rel_out = [rc(o_rel.at[:, col], o_rel.at[:, col], 11 + i, o) for i, o in enumerate((pc.buddy, pc.cross, pc.diag))]
    for c in rel_out:
        c.start()
    sc.wait_recv()
    sd.wait_recv()
    o_src[:, lanes(pc.s)] = (half[0].astype(F32) + halfx[0].astype(F32)).astype(BF)
    o_src[:, lanes(pc.cross)] = (half[1].astype(F32) + halfx[1].astype(F32)).astype(BF)
    se = rc(o_src.at[:, lanes(pc.s)], o_src.at[:, lanes(pc.s)], 9, pc.buddy)
    sf = rc(o_src.at[:, lanes(pc.cross)], o_src.at[:, lanes(pc.cross)], 10, pc.buddy)
    se.start()
    sf.start()
    for c in range(CH):
        across2[c].wait_recv()
        passed2[c].start()
    for c in range(CH):
        beside2[c].wait_recv()
        passed2[c].wait_recv()
    for c in (se, sf, *rel_out):
        c.wait_recv()

    for c in (ta, tb, tc, sa, sb, sc, sd, se, sf, ra, rb, *rel_out, *across, *beside, *passed, *across2, *beside2, *passed2):
        c.wait_send()
    for i in range(3):
        axis_wait(i, True)
    legs_sent(pc, recv1, s1, s2, r1)
    legs_sent(pc, recv3, s3, s4, r3)


def training_round(source_t, target_t, relation, sidx, tidx, kidx, counts, plan, inv):
    vm = pl.BlockSpec(memory_space=pltpu.VMEM)
    sm = pl.BlockSpec(memory_space=pltpu.SMEM)
    hb = pl.BlockSpec(memory_space=pl.ANY)
    dma = pltpu.SemaphoreType.DMA

    def bf(*shape):
        return pltpu.VMEM(shape, BF)

    def f(*shape):
        return pltpu.VMEM(shape, F32)

    tiles = bf(64, 16, 128)
    return pl.pallas_call(
        round_kernel,
        out_shape=(
            jax.ShapeDtypeStruct((D, ROWS), BF), jax.ShapeDtypeStruct((D, ROWS), BF), jax.ShapeDtypeStruct((REL, 512), F32),
        ),
        in_specs=[hb, hb, vm, vm, vm, vm, sm, sm, sm],
        out_specs=(vm, vm, vm),
        scratch_shapes=[
            f(D, Q), f(D, ROWS), bf(D, ROWS), bf(D, ROWS), bf(ROWS, EDGES), bf(ROWS, EDGES), bf(REL, EDGES),
            bf(D, EDGES), bf(D, EDGES), bf(D, EDGES), f(D, EDGES), bf(SPANS, E_CH, E_CH),
            bf(D, EDGES), bf(D, EDGES), bf(D, EDGES), bf(D, ROWS), bf(D, ROWS),
            bf(D, Q), tiles, tiles, bf(D, Q), tiles, tiles,
            bf(2, D, Q), bf(D, Q), bf(D, Q), bf(2, D, Q), bf(2, D, Q), bf(2, D, Q),
            f(REL, 512), f(REL, 512), f(REL, 512), f(REL, 512), f(3, 4, REL, 128),
            dma((2,)), dma((4,)), dma, dma, dma, dma, dma, dma, dma, dma,
            dma((3, CH)), dma((3, CH)), dma((3, CH)), dma((3, CH)), dma((14,)), dma((14,)), dma((3,)), dma((3,)),
        ],
        compiler_params=pltpu.CompilerParams(collective_id=0, has_side_effects=True, vmem_limit_bytes=56 << 20),
        name="training_round",
    )(source_t, target_t, relation, sidx, tidx, kidx, counts, plan, inv)


def adagrad_kernel(ws, ss, gs, wt, st, gt, wr, sr, gr, o_s, o_t, o_r):
    for w, s, g, o in ((ws, ss, gs, o_s), (wt, st, gt, o_t)):
        grad = g[...].astype(F32)
        total = s[...] + jnp.sum(grad * grad, axis=0, keepdims=True) * (1.0 / D)
        o[...] = w[...] - (LEARN_RATE * grad) / jnp.sqrt(total)

    @pl.when(pl.program_id(0) == 0)
    def _():
        grad = gr[:, 0:D]
        total = sr[...] + jnp.sum(grad * grad, axis=1, keepdims=True) * (1.0 / D)
        o_r[...] = wr[...] - (LEARN_RATE * grad) / jnp.sqrt(total)


def adagrad(ws, ss, gs, wt, st, gt, wr, sr, gr):
    n = 256
    tab = pl.BlockSpec((D, n), lambda i: (0, i))
    row = pl.BlockSpec((1, n), lambda i: (0, i))
    whole = lambda *s: pl.BlockSpec(s, lambda i: (0,) * len(s))
    return pl.pallas_call(
        adagrad_kernel,
        grid=(ROWS // n,),
        out_shape=(
            jax.ShapeDtypeStruct((D, ROWS), F32), jax.ShapeDtypeStruct((D, ROWS), F32), jax.ShapeDtypeStruct((REL, D), F32),
        ),
        in_specs=[tab, row, tab, tab, row, tab, whole(REL, D), whole(REL, 1), whole(REL, 512)],
        out_specs=(tab, tab, whole(REL, D)),
        compiler_params=pltpu.CompilerParams(vmem_limit_bytes=24 << 20),
        name="adagrad",
    )(ws, ss, gs, wt, st, gt, wr, sr, gr)


def per_device(source_table, target_table, source_state, target_state, relation, relation_state,
               plan, source_index, target_index, relation_index, edge_counts):
    source_t, target_t = source_table.T, target_table.T
    b = jnp.arange(64, dtype=jnp.int32)
    inv = jnp.sum(jnp.where(plan[None, :] == b[:, None], b[None, :], 0), axis=1)
    sg, tg, rg = training_round(
        source_t, target_t, relation, source_index, target_index, relation_index, edge_counts, plan, inv
    )
    ns, nt, nr = adagrad(
        source_t, source_state[None, :], sg, target_t, target_state[None, :], tg, relation, relation_state[:, None], rg
    )
    return ns.T, nt.T, nr


def solution(mesh):
    placed = (
        P("bucket", None), P("bucket", None), P("bucket"), P("bucket"), P(), P(), P(),
        P("bucket", "span"), P("bucket", "span"), P("bucket", "span"), P("bucket"),
    )
    return jax.shard_map(
        per_device,
        mesh=mesh,
        in_specs=placed,
        out_specs=(P("bucket", None), P("bucket", None), P()),
        check_vma=False,
    )
```

```python
import functools

import jax
import jax.numpy as jnp
from jax import lax
from jax.experimental import pallas as pl
from jax.experimental.pallas import tpu as pltpu
from jax.sharding import PartitionSpec as P

MESH = pl.DeviceIdType.MESH
BF = jnp.bfloat16
F32 = jnp.float32
E_CH = 640
LEARN_RATE = 0.25
NEG_WEIGHT = 0.03125
D = 400
HALF = 200
ROWS = 1024
Q = 256
EDGES = 2560
SPANS = 4
REL = 16
TILES = 50
CH = 5
CHROWS = D // CH
CHUNK = 512


class Place:
    def __init__(self):
        rem, div = lax.rem, lax.div
        self.me = lax.axis_index("bucket")
        self.s = lax.axis_index("span")
        self.x = div(self.me, 16)
        self.y = rem(div(self.me, 4), 4)
        self.z = rem(self.me, 4)
        self.zl = div(self.s, 2)
        self.core = rem(self.s, 2)
        self.buddy = self.s + 1 - 2 * self.core
        self.cross = rem(self.s + 2, 4)
        self.diag = rem(self.buddy + 2, 4)
        self.X = [rem(self.x + d, 4) for d in range(4)]
        self.Y = [rem(self.y + d, 4) for d in range(4)]
        self.Z = [rem(self.z + d, 4) for d in range(4)]
        way = 2 * self.zl - 1
        height = 2 * self.z + self.zl
        self.H = [rem(height + way * d + 8, 8) for d in range(4)]
        self.hz = [div(h, 2) for h in self.H]
        self.hs = [2 * rem(h, 2) + self.core for h in self.H]
        self.odd = [rem(d + 1 + self.zl, 2) for d in range(4)]
        self.U = [[rem(x + 2 * self.core + h, 4) for x in self.X] for h in self.H]
        self.row = 128 * self.U[0][0] + 32 * self.y + 16 * self.odd[0]
        self.relay = jnp.logical_or(self.U[0][0] < 3, jnp.logical_and(self.y == 0, self.odd[0] == 0))
        self.ds = [self.s, self.core, 2 - 2 * self.zl + self.core, 2 + self.core]
        self.dk = [0, 1 - self.zl, 1, self.zl]

    def greet(self):
        barrier = pltpu.get_barrier_semaphore()

        def hello(bucket, span):
            pl.semaphore_signal(barrier, inc=1, device_id=(bucket, span), device_id_type=MESH)

        beyond = rem8_pair(self)
        for dx in range(4):
            for dy in range(4):
                part = 16 * self.X[dx] + 4 * self.Y[dy]
                for d in range(4):
                    if dx or dy or d:
                        hello(part + self.hz[d], self.hs[d])
                hello(part + beyond, self.s)
        for o in (self.buddy, self.cross, self.diag):
            hello(self.me, o)
        hello(16 * self.x + 4 * self.y + self.Z[2], self.s)
        return barrier


GREETED = 63 + 16 + 3 + 1


def rem8_pair(pc):
    return lax.rem(pc.z + 1 + 2 * pc.zl, 4)


STEPS = (0, 1, 2, 1)
FAR_FIRST = sorted(
    ((dx, dy, d) for dx in range(4) for dy in range(4) for d in range(4)),
    key=lambda o: -(STEPS[o[0]] + STEPS[o[1]] + o[2]),
)


def tile_at(ref, row, lane):
    return ref.at[pl.ds(pl.multiple_of(row, 16), 16), pl.ds(pl.multiple_of(lane, 128), 128)]


def wait_tiles(buf, n, ssem, rsem, pc, send):
    ref = buf.at[pl.ds(0, n)]
    d = pltpu.make_async_remote_copy(
        src_ref=ref, dst_ref=ref, send_sem=ssem, recv_sem=rsem, device_id=(pc.me, pc.buddy), device_id_type=MESH
    )
    if send:
        d.wait_send()
    else:
        d.wait_recv()


def leg_one(pc, src, recv, sem_loc, ssem, rsem):
    for dx, dy, d in FAR_FIRST:
        if not (dx or dy or d):
            continue
        u = pc.U[d][dx]

        @pl.when(jnp.logical_or(u < 3, jnp.logical_and(pc.Y[dy] == 0, pc.odd[d] == 0)))
        def _():
            pltpu.make_async_remote_copy(
                src_ref=tile_at(src, 128 * u + 32 * pc.Y[dy] + 16 * pc.odd[d], 128 * (d // 2)),
                dst_ref=recv.at[pc.me], send_sem=ssem, recv_sem=rsem,
                device_id=(16 * pc.X[dx] + 4 * pc.Y[dy] + pc.hz[d], pc.hs[d]), device_id_type=MESH,
            ).start()

    @pl.when(pc.relay)
    def _():
        pltpu.make_async_copy(tile_at(src, pc.row, 0), recv.at[pc.me], sem_loc).start()


def leg_one_wait(pc, src, recv, sem_loc, ssem, rsem):
    @pl.when(pc.relay)
    def _():
        pltpu.make_async_copy(tile_at(src, pc.row, 0), recv.at[pc.me], sem_loc).wait()
        wait_tiles(recv, 63, ssem, rsem, pc, False)


def leg_two(pc, recv, pick, send, dst, sem_loc, ssem, rsem):
    @pl.when(pc.relay)
    def _():
        for i in range(64):
            send[i] = recv[pick(i)]
        for dx, dy, e in FAR_FIRST:
            if dx or dy or e:
                p = 16 * pc.X[dx] + 4 * pc.Y[dy] + pc.Z[e]
                pltpu.make_async_remote_copy(
                    src_ref=send.at[p], dst_ref=tile_at(dst, pc.row, Q * pc.ds[e] + 128 * pc.dk[e]),
                    send_sem=ssem, recv_sem=rsem, device_id=(p, pc.ds[e]), device_id_type=MESH,
                ).start()
        pltpu.make_async_copy(send.at[pc.me], tile_at(dst, pc.row, Q * pc.s), sem_loc).start()


def leg_two_wait(pc, recv, send, dst, sem_loc, ssem, rsem):
    @pl.when(pc.relay)
    def _():
        pltpu.make_async_copy(send.at[pc.me], tile_at(dst, pc.row, Q * pc.s), sem_loc).wait()
        wait_tiles(recv, TILES - 1, ssem, rsem, pc, False)

    @pl.when(jnp.logical_not(pc.relay))
    def _():
        wait_tiles(recv, TILES, ssem, rsem, pc, False)


def legs_sent(pc, recv, s1, s2, r1):
    @pl.when(pc.relay)
    def _():
        wait_tiles(recv, TILES - 1, s1, r1, pc, True)
        wait_tiles(recv, 63, s2, r1, pc, True)

    @pl.when(jnp.logical_not(pc.relay))
    def _():
        wait_tiles(recv, TILES, s1, r1, pc, True)


def lanes(q, n=Q):
    return pl.ds(pl.multiple_of(q * Q, Q), n)


def dot(a, b, ca=1, cb=0):
    return lax.dot_general(a, b, (((ca,), (cb,)), ((), ())), preferred_element_type=F32)


def quarter_rows(q):
    return pl.ds(pl.multiple_of(q * Q, Q), Q)


def chunk_at(c):
    return pl.ds(c * CHUNK if isinstance(c, int) else pl.multiple_of(c * CHUNK, CHUNK), CHUNK)


def alive_index(index, c, first, lim):
    slots = first + c * CHUNK + lax.broadcasted_iota(jnp.int32, (1, CHUNK), 1)
    return jnp.where(slots < lim[0], index, -1)


def group_column(core, g, z):
    t = lax.rem(g - z + 4, 4)
    upper = jnp.logical_and(t > 0, t < 3).astype(jnp.int32)
    second = (t > 1).astype(jnp.int32)
    return 4 * upper + 2 * core + second


def place_of_row(row, z):
    return 128 * group_column(row // 512, (row // 128) % 4, z) + row % 128


def round_kernel(
    src, tgt, rel_in, sidx_in, tidx_in, kidx_in, planrow_in, lim_in, plan_in,
    o_src, o_tgt, o_rel,
    rel, sidx, tidx, kidx, planrow, lim, plan,
    raw, src_raw, low, table, heads, tails, kinds, query, head, tail, relrow, coef, gtail, ghead, grel, tg, sg,
    send1, recv1, send2, quarter, recv3, send4,
    t1, t2send, t2, half, halfin, halfx, rg, r1buf, r2buf, r2send, rax, invcol, inv,
    sem_in, sem_loc, s1, r1, s2, r2, s3, r3, s4, r4, sag, rag, sbk, rbk, st, rt, srel, rrel,
):
    pc = Place()
    cin = []
    for k in range(2):
        g = lax.rem(pc.z + pc.zl + 3 * k - 2 * k * pc.zl, 4)
        at = pl.ds(pl.multiple_of(512 * pc.core + 128 * g, 128), 128)
        cin.append(pltpu.make_async_copy(tgt.at[:, at], raw.at[:, pl.ds(128 * k, 128)], sem_in.at[3 + k]))
    small = [
        pltpu.make_async_copy(a, b, sem_in.at[5 + i]) for i, (a, b) in enumerate((
            (rel_in, rel), (sidx_in, sidx), (tidx_in, tidx), (kidx_in, kidx), (planrow_in, planrow), (lim_in, lim), (plan_in, plan),
        ))
    ]
    csrc = pltpu.make_async_copy(src, src_raw, sem_in.at[1])
    for c in (*cin, *small, csrc):
        c.start()
    barrier = pc.greet()
    for c in cin:
        c.wait()
    send1[...] = raw[...].astype(BF)
    pl.semaphore_wait(barrier, GREETED)
    leg_one(pc, send1, recv1, sem_loc.at[0], s1, r1)

    first = pc.s * EDGES
    for c in small:
        c.wait()
    r = rel[...]
    hi = r.astype(BF)
    mid = (r - hi.astype(F32)).astype(BF)
    lo = (r - hi.astype(F32) - mid.astype(F32)).astype(BF)
    rel3 = jnp.concatenate([hi, mid, lo], axis=0)
    here = lax.broadcasted_iota(jnp.int32, (64, 64), 0) == planrow[...]
    found = jnp.sum(jnp.where(here, lax.broadcasted_iota(jnp.int32, (64, 64), 1), 0), axis=1, keepdims=True)
    invcol[...] = jnp.broadcast_to(jnp.minimum(found, 63), (64, 128))
    cinv = pltpu.make_async_copy(invcol, inv, sem_in.at[2])
    cinv.start()
    csrc.wait()
    low[...] = src_raw[...].astype(BF)

    def gather_heads(c, carry):
        at = chunk_at(c)
        rows = lax.broadcasted_iota(jnp.int32, (ROWS, CHUNK), 0)
        hot = (rows == alive_index(sidx[:, at], c, first, lim)).astype(F32).astype(BF)
        heads[:, at] = hot
        h = dot(low[...], hot)
        head[:, at] = h.astype(BF)
        k16 = lax.broadcasted_iota(jnp.int32, (REL, CHUNK), 0)
        khot = (k16 == alive_index(kidx[:, at], c, first, lim)).astype(F32).astype(BF)
        kinds[:, at] = khot
        rr = dot(rel3, jnp.concatenate([khot, khot, khot], axis=0), 0, 0)
        relrow[:, at] = rr
        hr, hm, kr, km = h[:HALF], h[HALF:], rr[:HALF], rr[HALF:]
        query[:, at] = jnp.concatenate([hr * kr - hm * km, hr * km + hm * kr], axis=0).astype(BF)
        return carry

    lax.fori_loop(0, EDGES // CHUNK, gather_heads, 0)
    cinv.wait()
    leg_one_wait(pc, send1, recv1, sem_loc.at[0], s1, r1)
    leg_two(pc, recv1, lambda i: plan[i], send2, table, sem_loc.at[1], s2, r2)

    def mark_tails(c, carry):
        rows = lax.broadcasted_iota(jnp.int32, (ROWS, CHUNK), 0)
        tails[:, chunk_at(c)] = (rows == alive_index(place_of_row(tidx[:, chunk_at(c)], pc.z), c, first, lim)).astype(F32).astype(BF)
        return carry

    lax.fori_loop(0, EDGES // CHUNK, mark_tails, 0)
    leg_two_wait(pc, recv1, send2, table, sem_loc.at[1], s2, r2)

    def cp(out, q, c, o, i, ss, rs):
        ref = out.at[pl.ds(c * CHROWS, CHROWS), lanes(q)]
        return pltpu.make_async_remote_copy(
            src_ref=ref, dst_ref=ref, send_sem=ss.at[i, c], recv_sem=rs.at[i, c],
            device_id=(pc.me, o), device_id_type=MESH,
        )

    across = [cp(table, pc.s, c, pc.cross, 0, sag, rag) for c in range(CH)]
    beside = [cp(table, pc.s, c, pc.buddy, 1, sag, rag) for c in range(CH)]
    passed = [cp(table, pc.cross, c, pc.buddy, 2, sag, rag) for c in range(CH)]
    for c in range(CH):
        across[c].start()
        beside[c].start()
    for c in range(CH):
        beside[c].wait_recv()
    near = pl.ds(pl.multiple_of(pc.zl * 512, 512), 512)
    far = pl.ds(pl.multiple_of(512 - pc.zl * 512, 512), 512)

    def tails_near(c, carry):
        tail[:, chunk_at(c)] = dot(table[:, near], tails[near, chunk_at(c)]).astype(BF)
        return carry

    for c in range(EDGES // CHUNK):
        tails_near(c, 0)
    for c in range(CH):
        across[c].wait_recv()
        passed[c].start()
    for c in range(CH):
        passed[c].wait_recv()

    def tails_far(c, carry):
        at = chunk_at(c)
        tail[:, at] = (tail[:, at].astype(F32) + dot(table[:, far], tails[far, at])).astype(BF)
        return carry

    for c in range(EDGES // CHUNK):
        tails_far(c, 0)

    def score_span(k, carry):
        base = pl.multiple_of(k * E_CH, 128)
        at = pl.ds(base, E_CH)
        for b in range(E_CH // 128):
            qb = query[:, pl.ds(pl.multiple_of(base + 128 * b, 128), 128)]
            score = dot(qb, tail[:, at], 0, 0)
            for j in range(E_CH // 128):
                u = score[:, 128 * j:128 * j + 128]
                if j == b:
                    one = lax.broadcasted_iota(jnp.int32, (128, 128), 0) == lax.broadcasted_iota(jnp.int32, (128, 128), 1)
                    w = jax.nn.sigmoid(jnp.where(one, -u, u)) * jnp.where(one, -1.0, NEG_WEIGHT)
                else:
                    w = jax.nn.sigmoid(u) * NEG_WEIGHT
                coef[k, pl.ds(128 * b, 128), pl.ds(128 * j, 128)] = w.astype(BF)
        gtail[:, at] = dot(query[:, at], coef[k]).astype(BF)
        return carry

    lax.fori_loop(0, SPANS, score_span, 0)

    def rc(src_ref, dst_ref, i, o):
        return pltpu.make_async_remote_copy(
            src_ref=src_ref, dst_ref=dst_ref, send_sem=st.at[i], recv_sem=rt.at[i], device_id=(pc.me, o), device_id_type=MESH
        )

    def to_bucket(src_ref, dst_ref, i, p):
        return pltpu.make_async_remote_copy(
            src_ref=src_ref, dst_ref=dst_ref, send_sem=srel.at[i], recv_sem=rrel.at[i], device_id=(p, pc.s), device_id_type=MESH
        )

    def target_sum(part):
        tg[:, part] = dot(gtail[...], tails[part, :], 1, 1).astype(BF)

    ta = rc(tg.at[:, lanes(pc.diag)], t1.at[1], 0, pc.buddy)
    tb = rc(tg.at[:, lanes(pc.buddy)], t1.at[0], 1, pc.buddy)
    tc = rc(t2send, t2, 5, pc.cross)
    target_sum(far)
    ta.start()
    target_sum(near)
    tb.start()
    ta.wait_recv()
    t2send[...] = (tg[:, lanes(pc.cross)].astype(F32) + t1[1].astype(F32)).astype(BF)
    tc.start()
    def query_span(k, carry):
        at = pl.ds(pl.multiple_of(k * E_CH, 128), E_CH)
        gq = dot(tail[:, at], coef[k], 1, 1)
        gr, gm = gq[:HALF], gq[HALF:]
        rr = relrow[:, at]
        kr, km = rr[:HALF], rr[HALF:]
        h = head[:, at].astype(F32)
        hr, hm = h[:HALF], h[HALF:]
        ghead[:, at] = jnp.concatenate([gr * kr + gm * km, gm * kr - gr * km], axis=0).astype(BF)
        grel[:, at] = jnp.concatenate([gr * hr + gm * hm, gm * hr - gr * hm], axis=0).astype(BF)
        return carry

    lax.fori_loop(0, SPANS, query_span, 0)

    def source_sum(part):
        sg[:, part] = dot(ghead[...], heads[part, :], 1, 1).astype(BF)

    sa = rc(sg.at[:, lanes(pc.buddy)], halfin.at[0], 2, pc.buddy)
    sb = rc(sg.at[:, lanes(pc.diag)], halfin.at[1], 3, pc.buddy)
    ra = rc(rg, r1buf, 4, pc.buddy)
    rg[:, 0:D] = dot(kinds[...], grel[...], 1, 1)
    rg[:, D:512] = jnp.zeros((REL, 512 - D), F32)
    ra.start()
    source_sum(near)
    sa.start()
    tb.wait_recv()
    tc.wait_recv()
    quarter[...] = (tg[:, lanes(pc.s)].astype(F32) + t1[0].astype(F32) + t2[...].astype(F32)).astype(BF)
    leg_one(pc, quarter, recv3, sem_loc.at[2], s3, r3)

    ra.wait_recv()
    r2send[...] = rg[...] + r1buf[...]
    rb = rc(r2send, r2buf, 6, pc.cross)
    rb.start()
    sc = rc(half.at[0], halfx.at[1], 7, pc.cross)
    sd = rc(half.at[1], halfx.at[0], 8, pc.cross)
    sa.wait_recv()
    half[0] = (sg[:, lanes(pc.s)].astype(F32) + halfin[0].astype(F32)).astype(BF)
    sc.start()
    source_sum(far)
    sb.start()
    sb.wait_recv()
    half[1] = (sg[:, lanes(pc.cross)].astype(F32) + halfin[1].astype(F32)).astype(BF)

    col = pl.ds(pl.multiple_of(pc.s * 128, 128), 128)
    px = [16 * x + 4 * pc.y + pc.z for x in pc.X[1:]]
    py = [16 * pc.x + 4 * y + pc.z for y in pc.Y[1:]]
    pz = [16 * pc.x + 4 * pc.y + z for z in pc.Z[1:]]

    def axis(i, coord, peers, total):
        rax[i, coord] = total
        for p in peers:
            to_bucket(rax.at[i, coord], rax.at[i, coord], i, p).start()

    def axis_wait(i, send=False):
        ref = rax.at[i, pl.ds(0, 3)]
        d = to_bucket(ref, ref, i, px[0])
        if send:
            d.wait_send()
            return None
        d.wait_recv()
        return (rax[i, 0] + rax[i, 1]) + (rax[i, 2] + rax[i, 3])

    rb.wait_recv()
    axis(0, pc.x, px, r2send[:, col] + r2buf[:, col])
    leg_one_wait(pc, quarter, recv3, sem_loc.at[2], s3, r3)
    leg_two(pc, recv3, lambda i: inv[i, 0], send4, o_tgt, sem_loc.at[3], s4, r4)
    sd.start()
    axis(1, pc.y, py, axis_wait(0))
    axis(2, pc.z, pz, axis_wait(1))

    leg_two_wait(pc, recv3, send4, o_tgt, sem_loc.at[3], s4, r4)
    across2 = [cp(o_tgt, pc.s, c, pc.cross, 0, sbk, rbk) for c in range(CH)]
    beside2 = [cp(o_tgt, pc.s, c, pc.buddy, 1, sbk, rbk) for c in range(CH)]
    passed2 = [cp(o_tgt, pc.cross, c, pc.buddy, 2, sbk, rbk) for c in range(CH)]
    for c in range(CH):
        across2[c].start()
        beside2[c].start()

    sc.wait_recv()
    sd.wait_recv()
    o_src[:, lanes(pc.s)] = (half[0].astype(F32) + halfx[0].astype(F32)).astype(BF)
    o_src[:, lanes(pc.cross)] = (half[1].astype(F32) + halfx[1].astype(F32)).astype(BF)
    se = rc(o_src.at[:, lanes(pc.s)], o_src.at[:, lanes(pc.s)], 9, pc.buddy)
    sf = rc(o_src.at[:, lanes(pc.cross)], o_src.at[:, lanes(pc.cross)], 10, pc.buddy)
    se.start()
    sf.start()
    for c in range(CH):
        across2[c].wait_recv()
        passed2[c].start()
    o_rel[:, col] = axis_wait(2)
    rel_out = [rc(o_rel.at[:, col], o_rel.at[:, col], 11 + i, o) for i, o in enumerate((pc.buddy, pc.cross, pc.diag))]
    for c in rel_out:
        c.start()
    for c in range(CH):
        beside2[c].wait_recv()
        passed2[c].wait_recv()
    for c in (se, sf, *rel_out):
        c.wait_recv()

    for c in (ta, tb, tc, sa, sb, sc, sd, se, sf, ra, rb, *rel_out, *across, *beside, *passed, *across2, *beside2, *passed2):
        c.wait_send()
    for i in range(3):
        axis_wait(i, True)
    legs_sent(pc, recv1, s1, s2, r1)
    legs_sent(pc, recv3, s3, s4, r3)


def training_round(source_t, target_t, relation, sidx, tidx, kidx, counts, plan):
    vm = pl.BlockSpec(memory_space=pltpu.VMEM)
    hb = pl.BlockSpec(memory_space=pltpu.HBM)
    dma = pltpu.SemaphoreType.DMA

    def i32(*shape):
        return pltpu.VMEM(shape, jnp.int32)

    def bf(*shape):
        return pltpu.VMEM(shape, BF)

    def f(*shape):
        return pltpu.VMEM(shape, F32)

    tiles = bf(64, 16, 128)
    kept = [
        pltpu.with_memory_space_constraint(a, pltpu.HBM) for a in (source_t, target_t, relation, sidx, tidx, kidx, plan[None, :])
    ]
    return pl.pallas_call(
        round_kernel,
        out_shape=(
            jax.ShapeDtypeStruct((D, ROWS), BF), jax.ShapeDtypeStruct((D, ROWS), BF), jax.ShapeDtypeStruct((REL, 512), F32),
        ),
        in_specs=[hb] * 9,
        out_specs=(vm, vm, vm),
        scratch_shapes=[
            f(REL, D), i32(1, EDGES), i32(1, EDGES), i32(1, EDGES), i32(1, 64), pltpu.SMEM((1,), jnp.int32), pltpu.SMEM((64,), jnp.int32),
            f(D, Q), f(D, ROWS), bf(D, ROWS), bf(D, ROWS), bf(ROWS, EDGES), bf(ROWS, EDGES), bf(REL, EDGES),
            bf(D, EDGES), bf(D, EDGES), bf(D, EDGES), f(D, EDGES), bf(SPANS, E_CH, E_CH),
            bf(D, EDGES), bf(D, EDGES), bf(D, EDGES), bf(D, ROWS), bf(D, ROWS),
            bf(D, Q), tiles, tiles, bf(D, Q), tiles, tiles,
            bf(2, D, Q), bf(D, Q), bf(D, Q), bf(2, D, Q), bf(2, D, Q), bf(2, D, Q),
            f(REL, 512), f(REL, 512), f(REL, 512), f(REL, 512), f(3, 4, REL, 128),
            pltpu.VMEM((64, 128), jnp.int32), pltpu.SMEM((64, 128), jnp.int32),
            dma((12,)), dma((4,)), dma, dma, dma, dma, dma, dma, dma, dma,
            dma((3, CH)), dma((3, CH)), dma((3, CH)), dma((3, CH)), dma((14,)), dma((14,)), dma((3,)), dma((3,)),
        ],
        compiler_params=pltpu.CompilerParams(collective_id=0, has_side_effects=True, vmem_limit_bytes=46 << 20),
        name="training_round",
    )(*kept, counts, pltpu.with_memory_space_constraint(plan, pltpu.HBM))


def adagrad_kernel(ws, ss, gs, wt, st, gt, wr, sr, gr, o_s, o_t, o_r, buf, sem):
    copies = []
    z = lax.rem(lax.axis_index("bucket"), 4)
    for i, (w, s, g, o) in enumerate(((ws, ss, gs, o_s), (wt, st, gt, o_t))):
        for q in range(ROWS // Q):
            at = pl.ds(q * Q, Q)
            if i == 0:
                grad = g[:, at].astype(F32)
            else:
                cols = [pl.multiple_of(128 * group_column(q // 2, 2 * (q % 2) + h, z), 128) for h in range(2)]
                grad = jnp.concatenate([g[:, pl.ds(c, 128)] for c in cols], axis=1).astype(F32)
            total = s[:, at] + jnp.sum(grad * grad, axis=0, keepdims=True) * (1.0 / D)
            buf[i, q] = w[:, at] - (LEARN_RATE * grad) / jnp.sqrt(total)
            copies.append(pltpu.make_async_copy(buf.at[i, q], o.at[:, at], sem.at[i, q]))
            copies[-1].start()
    grad = gr[:, 0:D]
    same = lax.broadcasted_iota(jnp.int32, (REL, REL), 0) == lax.broadcasted_iota(jnp.int32, (REL, REL), 1)
    state = jnp.sum(jnp.where(same, sr[...], 0.0), axis=1, keepdims=True)
    total = state + jnp.sum(grad * grad, axis=1, keepdims=True) * (1.0 / D)
    o_r[...] = wr[...] - (LEARN_RATE * grad) / jnp.sqrt(total)
    for c in copies:
        c.wait()


def adagrad(*args):
    vm = pl.BlockSpec(memory_space=pltpu.VMEM)
    hb = pl.BlockSpec(memory_space=pl.ANY)
    return pl.pallas_call(
        adagrad_kernel,
        out_shape=(
            jax.ShapeDtypeStruct((D, ROWS), F32), jax.ShapeDtypeStruct((D, ROWS), F32), jax.ShapeDtypeStruct((REL, D), F32),
        ),
        in_specs=[vm] * 9,
        out_specs=(hb, hb, vm),
        scratch_shapes=[pltpu.VMEM((2, ROWS // Q, D, Q), F32), pltpu.SemaphoreType.DMA((2, ROWS // Q))],
        compiler_params=pltpu.CompilerParams(vmem_limit_bytes=24 << 20),
        name="adagrad",
    )(*args)


def per_device(source_table, target_table, source_state, target_state, relation, relation_state,
               plan, source_index, target_index, relation_index, edge_counts):
    source_t, target_t = source_table.T, target_table.T
    sg, tg, rg = training_round(
        source_t, target_t, relation, source_index, target_index, relation_index, edge_counts, plan
    )
    ns, nt, nr = adagrad(
        source_t, source_state[None, :], sg, target_t, target_state[None, :], tg, relation, relation_state[None, :], rg
    )
    return ns.T, nt.T, nr


def solution(mesh):
    placed = (
        P("bucket", None), P("bucket", None), P("bucket"), P("bucket"), P(), P(), P(),
        P("bucket", "span"), P("bucket", "span"), P("bucket", "span"), P("bucket"),
    )
    return jax.shard_map(
        per_device,
        mesh=mesh,
        in_specs=placed,
        out_specs=(P("bucket", None), P("bucket", None), P()),
        check_vma=False,
    )
```

```python
import functools

import jax
import jax.numpy as jnp
from jax import lax
from jax.experimental import pallas as pl
from jax.experimental.pallas import tpu as pltpu
from jax.sharding import PartitionSpec as P

MESH = pl.DeviceIdType.MESH
BF = jnp.bfloat16
F32 = jnp.float32
E_CH = 640
LEARN_RATE = 0.25
NEG_WEIGHT = 0.03125
D = 400
HALF = 200
ROWS = 1024
Q = 256
EDGES = 2560
SPANS = 4
REL = 16
TILES = 50
PIECES = ((0, 0, 208), (0, 208, 192), (1, 0, 208), (1, 208, 192))
CH = len(PIECES)
CHUNK = 512


class Place:
    def __init__(self):
        rem, div = lax.rem, lax.div
        self.me = lax.axis_index("bucket")
        self.s = lax.axis_index("span")
        self.x = div(self.me, 16)
        self.y = rem(div(self.me, 4), 4)
        self.z = rem(self.me, 4)
        self.zl = div(self.s, 2)
        self.core = rem(self.s, 2)
        self.buddy = self.s + 1 - 2 * self.core
        self.cross = rem(self.s + 2, 4)
        self.diag = rem(self.buddy + 2, 4)
        self.X = [rem(self.x + d, 4) for d in range(4)]
        self.Y = [rem(self.y + d, 4) for d in range(4)]
        self.Z = [rem(self.z + d, 4) for d in range(4)]
        way = 2 * self.zl - 1
        height = 2 * self.z + self.zl
        self.H = [rem(height + way * d + 8, 8) for d in range(4)]
        self.hz = [div(h, 2) for h in self.H]
        self.hs = [2 * rem(h, 2) + self.core for h in self.H]
        self.odd = [rem(d + 1 + self.zl, 2) for d in range(4)]
        self.U = [[rem(x + 2 * self.core + h, 4) for x in self.X] for h in self.H]
        self.row = 128 * self.U[0][0] + 32 * self.y + 16 * self.odd[0]
        self.relay = jnp.logical_or(self.U[0][0] < 3, jnp.logical_and(self.y == 0, self.odd[0] == 0))
        self.ds = [self.s, self.core, 2 - 2 * self.zl + self.core, 2 + self.core]
        self.dk = [0, 1 - self.zl, 1, self.zl]

    def greet(self):
        barrier = pltpu.get_barrier_semaphore()

        def hello(bucket, span):
            pl.semaphore_signal(barrier, inc=1, device_id=(bucket, span), device_id_type=MESH)

        beyond = rem8_pair(self)
        for dx, dy, d in FAR_FIRST:
            part = 16 * self.X[dx] + 4 * self.Y[dy]
            if dx or dy or d:
                hello(part + self.hz[d], self.hs[d])
            if d == 2:
                hello(part + beyond, self.s)
        for o in (self.buddy, self.cross, self.diag):
            hello(self.me, o)
        hello(16 * self.x + 4 * self.y + self.Z[2], self.s)
        return barrier


GREETED = 63 + 16 + 3 + 1


def rem8_pair(pc):
    return lax.rem(pc.z + 1 + 2 * pc.zl, 4)


STEPS = (0, 1, 2, 1)
FAR_FIRST = sorted(
    ((dx, dy, d) for dx in range(4) for dy in range(4) for d in range(4)),
    key=lambda o: -(STEPS[o[0]] + STEPS[o[1]] + o[2]),
)


def tile_at(ref, row, lane):
    return ref.at[pl.ds(pl.multiple_of(row, 16), 16), pl.ds(pl.multiple_of(lane, 128), 128)]


def wait_tiles(buf, n, ssem, rsem, pc, send):
    ref = buf.at[pl.ds(0, n)]
    d = pltpu.make_async_remote_copy(
        src_ref=ref, dst_ref=ref, send_sem=ssem, recv_sem=rsem, device_id=(pc.me, pc.buddy), device_id_type=MESH
    )
    if send:
        d.wait_send()
    else:
        d.wait_recv()


def leg_one(pc, src, recv, sem_loc, ssem, rsem, columns=(0, 1)):
    for dx, dy, d in FAR_FIRST:
        if not (dx or dy or d) or d // 2 not in columns:
            continue
        u = pc.U[d][dx]

        @pl.when(jnp.logical_or(u < 3, jnp.logical_and(pc.Y[dy] == 0, pc.odd[d] == 0)))
        def _():
            pltpu.make_async_remote_copy(
                src_ref=tile_at(src, 128 * u + 32 * pc.Y[dy] + 16 * pc.odd[d], 128 * (d // 2)),
                dst_ref=recv.at[pc.me], send_sem=ssem, recv_sem=rsem,
                device_id=(16 * pc.X[dx] + 4 * pc.Y[dy] + pc.hz[d], pc.hs[d]), device_id_type=MESH,
            ).start()

    if 0 in columns:
        @pl.when(pc.relay)
        def _():
            pltpu.make_async_copy(tile_at(src, pc.row, 0), recv.at[pc.me], sem_loc).start()


def leg_one_wait(pc, src, recv, sem_loc, ssem, rsem):
    @pl.when(pc.relay)
    def _():
        pltpu.make_async_copy(tile_at(src, pc.row, 0), recv.at[pc.me], sem_loc).wait()
        wait_tiles(recv, 63, ssem, rsem, pc, False)


def leg_two(pc, recv, pick, send, dst, sem_loc, ssem, rsem):
    @pl.when(pc.relay)
    def _():
        for i in range(64):
            send[i] = recv[pick(i)]
        for dx, dy, e in FAR_FIRST:
            if dx or dy or e:
                p = 16 * pc.X[dx] + 4 * pc.Y[dy] + pc.Z[e]
                pltpu.make_async_remote_copy(
                    src_ref=send.at[p], dst_ref=tile_at(dst, pc.row, Q * pc.ds[e] + 128 * pc.dk[e]),
                    send_sem=ssem, recv_sem=rsem.at[pc.dk[e]], device_id=(p, pc.ds[e]), device_id_type=MESH,
                ).start()
        pltpu.make_async_copy(send.at[pc.me], tile_at(dst, pc.row, Q * pc.s), sem_loc).start()


def leg_two_wait(pc, recv, send, dst, sem_loc, ssem, rsem, column):
    if column:
        wait_tiles(recv, TILES // 2, ssem, rsem.at[1], pc, False)
        return

    @pl.when(pc.relay)
    def _():
        pltpu.make_async_copy(send.at[pc.me], tile_at(dst, pc.row, Q * pc.s), sem_loc).wait()
        wait_tiles(recv, TILES // 2 - 1, ssem, rsem.at[0], pc, False)

    @pl.when(jnp.logical_not(pc.relay))
    def _():
        wait_tiles(recv, TILES // 2, ssem, rsem.at[0], pc, False)


def legs_sent(pc, recv, s1, s2, r1):
    @pl.when(pc.relay)
    def _():
        wait_tiles(recv, TILES - 1, s1, r1, pc, True)
        wait_tiles(recv, 63, s2, r1, pc, True)

    @pl.when(jnp.logical_not(pc.relay))
    def _():
        wait_tiles(recv, TILES, s1, r1, pc, True)


def lanes(q, n=Q):
    return pl.ds(pl.multiple_of(q * Q, Q), n)


def dot(a, b, ca=1, cb=0):
    return lax.dot_general(a, b, (((ca,), (cb,)), ((), ())), preferred_element_type=F32)


def quarter_rows(q):
    return pl.ds(pl.multiple_of(q * Q, Q), Q)


def chunk_at(c):
    return pl.ds(c * CHUNK if isinstance(c, int) else pl.multiple_of(c * CHUNK, CHUNK), CHUNK)


def alive_index(index, c, first, lim):
    slots = first + c * CHUNK + lax.broadcasted_iota(jnp.int32, (1, CHUNK), 1)
    return jnp.where(slots < lim[0], index, -1)


def group_column(core, g, z):
    t = lax.rem(g - z + 4, 4)
    upper = jnp.logical_and(t > 0, t < 3).astype(jnp.int32)
    second = (t > 1).astype(jnp.int32)
    return 4 * upper + 2 * core + second


def place_of_row(row, z):
    return 128 * group_column(row // 512, (row // 128) % 4, z) + row % 128


def round_kernel(
    src, tgt, rel_in, sidx_in, tidx_in, kidx_in, planrow_in, lim, plan_in, state_in,
    o_new, o_tgt, o_rel,
    rel, sidx, tidx, kidx, planrow, plan, state, o_src,
    raw, src_raw, low, table, heads, tails, kinds, query, head, tail, relrow, coef, gtail, ghead, grel, tg, sg,
    send1, recv1, send2, quarter, recv3, send4,
    t1, t2send, t2, half, halfin, halfx, rg, r1buf, r2buf, r2send, rax, invcol, inv,
    sem_in, sem_loc, s1, r1, s2, r2, s3, r3, s4, r4, sag, rag, sbk, rbk, st, rt, srel, rrel,
):
    pc = Place()
    barrier = pc.greet()
    cin = []
    for k in range(2):
        g = lax.rem(pc.z + pc.zl + 3 * k - 2 * k * pc.zl, 4)
        at = pl.ds(pl.multiple_of(512 * pc.core + 128 * g, 128), 128)
        cin.append(pltpu.make_async_copy(tgt.at[:, at], raw.at[:, pl.ds(128 * k, 128)], sem_in.at[3 + k]))
    small = [
        pltpu.make_async_copy(a, b, sem_in.at[5 + i]) for i, (a, b) in enumerate((
            (rel_in, rel), (sidx_in, sidx), (tidx_in, tidx), (kidx_in, kidx), (planrow_in, planrow), (plan_in, plan), (state_in, state),
        ))
    ]
    csrc = pltpu.make_async_copy(src, src_raw, sem_in.at[1])
    for c in (*cin, *small, csrc):
        c.start()
    for c in cin:
        c.wait()
    send1[...] = raw[...].astype(BF)
    pl.semaphore_wait(barrier, GREETED)
    leg_one(pc, send1, recv1, sem_loc.at[0], s1, r1)

    first = pc.s * EDGES
    for c in small:
        c.wait()
    r = rel[...]
    hi = r.astype(BF)
    mid = (r - hi.astype(F32)).astype(BF)
    lo = (r - hi.astype(F32) - mid.astype(F32)).astype(BF)
    rel3 = jnp.concatenate([hi, mid, lo], axis=0)
    here = lax.broadcasted_iota(jnp.int32, (64, 64), 0) == planrow[...]
    found = jnp.sum(jnp.where(here, lax.broadcasted_iota(jnp.int32, (64, 64), 1), 0), axis=1, keepdims=True)
    invcol[...] = jnp.broadcast_to(jnp.minimum(found, 63), (64, 128))
    cinv = pltpu.make_async_copy(invcol, inv, sem_in.at[2])
    cinv.start()
    csrc.wait()
    low[...] = src_raw[...].astype(BF)

    def gather_heads(c, carry):
        at = chunk_at(c)
        rows = lax.broadcasted_iota(jnp.int32, (ROWS, CHUNK), 0)
        hot = (rows == alive_index(sidx[:, at], c, first, lim)).astype(F32).astype(BF)
        heads[:, at] = hot
        h = dot(low[...], hot)
        head[:, at] = h.astype(BF)
        k16 = lax.broadcasted_iota(jnp.int32, (REL, CHUNK), 0)
        khot = (k16 == alive_index(kidx[:, at], c, first, lim)).astype(F32).astype(BF)
        kinds[:, at] = khot
        rr = dot(rel3, jnp.concatenate([khot, khot, khot], axis=0), 0, 0)
        relrow[:, at] = rr
        hr, hm, kr, km = h[:HALF], h[HALF:], rr[:HALF], rr[HALF:]
        query[:, at] = jnp.concatenate([hr * kr - hm * km, hr * km + hm * kr], axis=0).astype(BF)
        return carry

    lax.fori_loop(0, EDGES // CHUNK, gather_heads, 0)
    cinv.wait()
    leg_one_wait(pc, send1, recv1, sem_loc.at[0], s1, r1)
    leg_two(pc, recv1, lambda i: plan[i], send2, table, sem_loc.at[1], s2, r2)

    def mark_tails(c, carry):
        rows = lax.broadcasted_iota(jnp.int32, (ROWS, CHUNK), 0)
        tails[:, chunk_at(c)] = (rows == alive_index(place_of_row(tidx[:, chunk_at(c)], pc.z), c, first, lim)).astype(F32).astype(BF)
        return carry

    lax.fori_loop(0, EDGES // CHUNK, mark_tails, 0)
    def cp(out, q, c, o, i, ss, rs):
        k, row, rows = PIECES[c]
        ref = out.at[pl.ds(row, rows), pl.ds(pl.multiple_of(q * Q + 128 * k, 128), 128)]
        return pltpu.make_async_remote_copy(
            src_ref=ref, dst_ref=ref, send_sem=ss.at[i, c], recv_sem=rs.at[i, c],
            device_id=(pc.me, o), device_id_type=MESH,
        )

    def spread(out, ss, rs):
        across = [cp(out, pc.s, c, pc.cross, 0, ss, rs) for c in range(CH)]
        beside = [cp(out, pc.s, c, pc.buddy, 1, ss, rs) for c in range(CH)]
        passed = [cp(out, pc.cross, c, pc.buddy, 2, ss, rs) for c in range(CH)]
        return across, beside, passed

    across, beside, passed = spread(table, sag, rag)
    for k in range(2):
        leg_two_wait(pc, recv1, send2, table, sem_loc.at[1], s2, r2, k)
        for c in range(2 * k, 2 * k + 2):
            across[c].start()
            beside[c].start()
    for c in range(CH):
        beside[c].wait_recv()
    near = pl.ds(pl.multiple_of(pc.zl * 512, 512), 512)
    far = pl.ds(pl.multiple_of(512 - pc.zl * 512, 512), 512)


    def tails_near(c, carry):
        tail[:, chunk_at(c)] = dot(table[:, near], tails[near, chunk_at(c)]).astype(BF)
        return carry

    for c in range(EDGES // CHUNK):
        tails_near(c, 0)
    for c in range(CH):
        across[c].wait_recv()
        passed[c].start()
    for c in range(CH):
        passed[c].wait_recv()

    def tails_far(c, carry):
        at = chunk_at(c)
        tail[:, at] = (tail[:, at].astype(F32) + dot(table[:, far], tails[far, at])).astype(BF)
        return carry

    for c in range(EDGES // CHUNK):
        tails_far(c, 0)

    def score_span(k, carry):
        base = pl.multiple_of(k * E_CH, 128)
        at = pl.ds(base, E_CH)
        score = dot(query[:, at], tail[:, at], 0, 0)
        for b in range(E_CH // 128):
            for j in range(E_CH // 128):
                bend = jnp.tanh(0.5 * score[128 * b:128 * b + 128, 128 * j:128 * j + 128])
                w = (0.5 * NEG_WEIGHT) * bend + 0.5 * NEG_WEIGHT
                if j == b:
                    one = lax.broadcasted_iota(jnp.int32, (128, 128), 0) == lax.broadcasted_iota(jnp.int32, (128, 128), 1)
                    w = jnp.where(one, 0.5 * bend - 0.5, w)
                coef[k, pl.ds(128 * b, 128), pl.ds(128 * j, 128)] = w.astype(BF)
        gtail[:, at] = dot(query[:, at], coef[k]).astype(BF)
        return carry

    lax.fori_loop(0, SPANS, score_span, 0)

    def rc(src_ref, dst_ref, i, o):
        return pltpu.make_async_remote_copy(
            src_ref=src_ref, dst_ref=dst_ref, send_sem=st.at[i], recv_sem=rt.at[i], device_id=(pc.me, o), device_id_type=MESH
        )

    def to_bucket(src_ref, dst_ref, i, p):
        return pltpu.make_async_remote_copy(
            src_ref=src_ref, dst_ref=dst_ref, send_sem=srel.at[i], recv_sem=rrel.at[i], device_id=(p, pc.s), device_id_type=MESH
        )

    def target_sum(part):
        tg[:, part] = dot(gtail[...], tails[part, :], 1, 1).astype(BF)

    ta = rc(tg.at[:, lanes(pc.diag)], t1.at[1], 0, pc.buddy)
    tb = rc(tg.at[:, lanes(pc.buddy)], t1.at[0], 1, pc.buddy)
    tc = [rc(t2send.at[:, pl.ds(128 * k, 128)], t2.at[:, pl.ds(128 * k, 128)], 5 + 9 * k, pc.cross) for k in range(2)]
    target_sum(far)
    ta.start()
    target_sum(near)
    tb.start()
    ta.wait_recv()
    t2send[...] = (tg[:, lanes(pc.cross)].astype(F32) + t1[1].astype(F32)).astype(BF)
    tc[1].start()
    tc[0].start()
    def query_span(k, carry):
        at = pl.ds(pl.multiple_of(k * E_CH, 128), E_CH)
        gq = dot(tail[:, at], coef[k], 1, 1)
        gr, gm = gq[:HALF], gq[HALF:]
        rr = relrow[:, at]
        kr, km = rr[:HALF], rr[HALF:]
        h = head[:, at].astype(F32)
        hr, hm = h[:HALF], h[HALF:]
        ghead[:, at] = jnp.concatenate([gr * kr + gm * km, gm * kr - gr * km], axis=0).astype(BF)
        grel[:, at] = jnp.concatenate([gr * hr + gm * hm, gm * hr - gr * hm], axis=0).astype(BF)
        return carry

    lax.fori_loop(0, SPANS, query_span, 0)

    def source_sum(part):
        sg[:, part] = dot(ghead[...], heads[part, :], 1, 1).astype(BF)

    sa = rc(sg.at[:, lanes(pc.buddy)], halfin.at[0], 2, pc.buddy)
    sb = rc(sg.at[:, lanes(pc.diag)], halfin.at[1], 3, pc.buddy)
    ra = rc(rg, r1buf, 4, pc.buddy)
    def quarter_column(k):
        tc[k].wait_recv()
        at = pl.ds(pl.multiple_of(pc.s * Q + 128 * k, 128), 128)
        col = pl.ds(128 * k, 128)
        quarter[:, col] = (tg[:, at].astype(F32) + t1[0, :, col].astype(F32) + t2[:, col].astype(F32)).astype(BF)
        leg_one(pc, quarter, recv3, sem_loc.at[2], s3, r3, (k,))

    sc = rc(half.at[0], halfx.at[1], 7, pc.cross)
    sd = rc(half.at[1], halfx.at[0], 8, pc.cross)
    source_sum(near)
    sa.start()
    tb.wait_recv()
    quarter_column(1)
    rg[:, 0:D] = dot(kinds[...], grel[...], 1, 1)
    rg[:, D:512] = jnp.zeros((REL, 512 - D), F32)
    ra.start()
    quarter_column(0)
    ra.wait_recv()
    r2send[...] = rg[...] + r1buf[...]
    rb = rc(r2send, r2buf, 6, pc.cross)
    rb.start()
    sa.wait_recv()
    half[0] = (sg[:, lanes(pc.s)].astype(F32) + halfin[0].astype(F32)).astype(BF)
    sc.start()
    source_sum(far)
    sb.start()

    col = pl.ds(pl.multiple_of(pc.s * 128, 128), 128)
    px = [16 * x + 4 * pc.y + pc.z for x in pc.X[1:]]
    py = [16 * pc.x + 4 * y + pc.z for y in pc.Y[1:]]
    pz = [16 * pc.x + 4 * pc.y + z for z in pc.Z[1:]]

    def axis(i, coord, peers, total):
        rax[i, coord] = total
        for p in peers:
            to_bucket(rax.at[i, coord], rax.at[i, coord], i, p).start()

    def axis_wait(i, send=False):
        ref = rax.at[i, pl.ds(0, 3)]
        d = to_bucket(ref, ref, i, px[0])
        if send:
            d.wait_send()
            return None
        d.wait_recv()
        return (rax[i, 0] + rax[i, 1]) + (rax[i, 2] + rax[i, 3])

    sb.wait_recv()
    half[1] = (sg[:, lanes(pc.cross)].astype(F32) + halfin[1].astype(F32)).astype(BF)
    sd.start()
    rb.wait_recv()
    axis(0, pc.x, px, r2send[:, col] + r2buf[:, col])
    leg_one_wait(pc, quarter, recv3, sem_loc.at[2], s3, r3)
    leg_two(pc, recv3, lambda i: inv[i, 0], send4, o_tgt, sem_loc.at[3], s4, r4)
    axis(1, pc.y, py, axis_wait(0))
    axis(2, pc.z, pz, axis_wait(1))
    across2, beside2, passed2 = spread(o_tgt, sbk, rbk)
    for k in range(2):
        leg_two_wait(pc, recv3, send4, o_tgt, sem_loc.at[3], s4, r4, k)
        for c in range(2 * k, 2 * k + 2):
            across2[c].start()
            beside2[c].start()
    sc.wait_recv()
    sd.wait_recv()
    def source_step(q):
        at = lanes(q)
        grad = o_src[:, at].astype(F32)
        total = state[:, at] + jnp.sum(grad * grad, axis=0, keepdims=True) * (1.0 / D)
        o_new[:, at] = src_raw[:, at] - grad * (LEARN_RATE / jnp.sqrt(total))

    o_src[:, lanes(pc.s)] = (half[0].astype(F32) + halfx[0].astype(F32)).astype(BF)
    o_src[:, lanes(pc.cross)] = (half[1].astype(F32) + halfx[1].astype(F32)).astype(BF)
    se = rc(o_src.at[:, lanes(pc.s)], o_src.at[:, lanes(pc.s)], 9, pc.buddy)
    sf = rc(o_src.at[:, lanes(pc.cross)], o_src.at[:, lanes(pc.cross)], 10, pc.buddy)
    se.start()
    sf.start()
    o_rel[:, col] = axis_wait(2)
    rel_out = [rc(o_rel.at[:, col], o_rel.at[:, col], 11 + i, o) for i, o in enumerate((pc.buddy, pc.cross, pc.diag))]
    for c in rel_out:
        c.start()
    source_step(pc.s)
    source_step(pc.cross)
    for c in range(CH):
        across2[c].wait_recv()
        passed2[c].start()
    se.wait_recv()
    sf.wait_recv()
    source_step(pc.buddy)
    source_step(pc.diag)
    for c in range(CH):
        beside2[c].wait_recv()
        passed2[c].wait_recv()
    for c in rel_out:
        c.wait_recv()

    for c in (ta, tb, *tc, sa, sb, sc, sd, se, sf, ra, rb, *rel_out, *across, *beside, *passed, *across2, *beside2, *passed2):
        c.wait_send()
    for i in range(3):
        axis_wait(i, True)
    legs_sent(pc, recv1, s1, s2, r1)
    legs_sent(pc, recv3, s3, s4, r3)


def training_round(source_t, target_t, relation, sidx, tidx, kidx, counts, plan, state):
    vm = pl.BlockSpec(memory_space=pltpu.VMEM)
    hb = pl.BlockSpec(memory_space=pltpu.HBM)
    dma = pltpu.SemaphoreType.DMA

    def i32(*shape):
        return pltpu.VMEM(shape, jnp.int32)

    def bf(*shape):
        return pltpu.VMEM(shape, BF)

    def f(*shape):
        return pltpu.VMEM(shape, F32)

    tiles = bf(64, 16, 128)
    kept = [
        pltpu.with_memory_space_constraint(a, pltpu.HBM) for a in (source_t, target_t, relation, sidx, tidx, kidx, plan[None, :], plan, state)
    ]
    return pl.pallas_call(
        round_kernel,
        out_shape=(
            jax.ShapeDtypeStruct((D, ROWS), F32), jax.ShapeDtypeStruct((D, ROWS), BF), jax.ShapeDtypeStruct((REL, 512), F32),
        ),
        in_specs=[hb] * 7 + [pl.BlockSpec(memory_space=pltpu.SMEM)] + [hb] * 2,
        out_specs=(vm, vm, vm),
        scratch_shapes=[
            f(REL, D), i32(1, EDGES), i32(1, EDGES), i32(1, EDGES), i32(1, 64), pltpu.SMEM((64,), jnp.int32), f(1, ROWS), bf(D, ROWS),
            f(D, Q), f(D, ROWS), bf(D, ROWS), bf(D, ROWS), bf(ROWS, EDGES), bf(ROWS, EDGES), bf(REL, EDGES),
            bf(D, EDGES), bf(D, EDGES), bf(D, EDGES), f(D, EDGES), bf(SPANS, E_CH, E_CH),
            bf(D, EDGES), bf(D, EDGES), bf(D, EDGES), bf(D, ROWS), bf(D, ROWS),
            bf(D, Q), tiles, tiles, bf(D, Q), tiles, tiles,
            bf(2, D, Q), bf(D, Q), bf(D, Q), bf(2, D, Q), bf(2, D, Q), bf(2, D, Q),
            f(REL, 512), f(REL, 512), f(REL, 512), f(REL, 512), f(3, 4, REL, 128),
            pltpu.VMEM((64, 128), jnp.int32), pltpu.SMEM((64, 128), jnp.int32),
            dma((13,)), dma((4,)), dma, dma, dma, dma((2,)), dma, dma, dma, dma((2,)),
            dma((3, CH)), dma((3, CH)), dma((3, CH)), dma((3, CH)), dma((15,)), dma((15,)), dma((3,)), dma((3,)),
        ],
        compiler_params=pltpu.CompilerParams(collective_id=0, has_side_effects=True, vmem_limit_bytes=46 << 20),
        name="training_round",
    )(*kept[:7], counts, *kept[7:])


def adagrad_kernel(new, wt, st, gt, wr, sr, gr, o_s, o_t, o_r, buf, sem):
    copies = [pltpu.make_async_copy(new, o_s, sem.at[ROWS // Q])]
    copies[0].start()
    z = lax.rem(lax.axis_index("bucket"), 4)
    for q in range(ROWS // Q):
        at = pl.ds(q * Q, Q)
        cols = [pl.multiple_of(128 * group_column(q // 2, 2 * (q % 2) + h, z), 128) for h in range(2)]
        grad = jnp.concatenate([gt[:, pl.ds(c, 128)] for c in cols], axis=1).astype(F32)
        total = st[:, at] + jnp.sum(grad * grad, axis=0, keepdims=True) * (1.0 / D)
        buf[q] = wt[:, at] - grad * (LEARN_RATE / jnp.sqrt(total))
        copies.append(pltpu.make_async_copy(buf.at[q], o_t.at[:, at], sem.at[q]))
        copies[-1].start()
    grad = gr[:, 0:D]
    same = lax.broadcasted_iota(jnp.int32, (REL, REL), 0) == lax.broadcasted_iota(jnp.int32, (REL, REL), 1)
    state = jnp.sum(jnp.where(same, sr[...], 0.0), axis=1, keepdims=True)
    total = state + jnp.sum(grad * grad, axis=1, keepdims=True) * (1.0 / D)
    o_r[...] = wr[...] - grad * (LEARN_RATE / jnp.sqrt(total))
    for c in copies:
        c.wait()


def adagrad(*args):
    vm = pl.BlockSpec(memory_space=pltpu.VMEM)
    hb = pl.BlockSpec(memory_space=pl.ANY)
    return pl.pallas_call(
        adagrad_kernel,
        out_shape=(
            jax.ShapeDtypeStruct((D, ROWS), F32), jax.ShapeDtypeStruct((D, ROWS), F32), jax.ShapeDtypeStruct((REL, D), F32),
        ),
        in_specs=[vm] * 7,
        out_specs=(hb, hb, vm),
        scratch_shapes=[pltpu.VMEM((ROWS // Q, D, Q), F32), pltpu.SemaphoreType.DMA((ROWS // Q + 1,))],
        compiler_params=pltpu.CompilerParams(vmem_limit_bytes=24 << 20),
        name="adagrad",
    )(*args)


def per_device(source_table, target_table, source_state, target_state, relation, relation_state,
               plan, source_index, target_index, relation_index, edge_counts):
    source_t, target_t = source_table.T, target_table.T
    new, tg, rg = training_round(
        source_t, target_t, relation, source_index, target_index, relation_index, edge_counts, plan, source_state[None, :]
    )
    ns, nt, nr = adagrad(new, target_t, target_state[None, :], tg, relation, relation_state[None, :], rg)
    return ns.T, nt.T, nr


def solution(mesh):
    placed = (
        P("bucket", None), P("bucket", None), P("bucket"), P("bucket"), P(), P(), P(),
        P("bucket", "span"), P("bucket", "span"), P("bucket", "span"), P("bucket"),
    )
    return jax.shard_map(
        per_device,
        mesh=mesh,
        in_specs=placed,
        out_specs=(P("bucket", None), P("bucket", None), P()),
        check_vma=False,
    )
```

```python
import functools

import jax
import jax.numpy as jnp
from jax import lax
from jax.experimental import pallas as pl
from jax.experimental.pallas import tpu as pltpu
from jax.sharding import PartitionSpec as P

MESH = pl.DeviceIdType.MESH
BF = jnp.bfloat16
F32 = jnp.float32
E_CH = 640
LEARN_RATE = 0.25
NEG_WEIGHT = 0.03125
D = 400
HALF = 200
ROWS = 1024
Q = 256
EDGES = 2560
SPANS = 4
REL = 16
TILES = 50
PIECES = ((0, 0, 208), (0, 208, 192), (1, 0, 208), (1, 208, 192))
CH = len(PIECES)
CHUNK = 512


class Place:
    def __init__(self):
        rem, div = lax.rem, lax.div
        self.me = lax.axis_index("bucket")
        self.s = lax.axis_index("span")
        self.x = div(self.me, 16)
        self.y = rem(div(self.me, 4), 4)
        self.z = rem(self.me, 4)
        self.zl = div(self.s, 2)
        self.core = rem(self.s, 2)
        self.buddy = self.s + 1 - 2 * self.core
        self.cross = rem(self.s + 2, 4)
        self.diag = rem(self.buddy + 2, 4)
        self.X = [rem(self.x + d, 4) for d in range(4)]
        self.Y = [rem(self.y + d, 4) for d in range(4)]
        self.Z = [rem(self.z + d, 4) for d in range(4)]
        way = 2 * self.zl - 1
        height = 2 * self.z + self.zl
        self.H = [rem(height + way * d + 8, 8) for d in range(4)]
        self.hz = [div(h, 2) for h in self.H]
        self.hs = [2 * rem(h, 2) + self.core for h in self.H]
        self.odd = [rem(d + 1 + self.zl, 2) for d in range(4)]
        self.U = [[rem(x + 2 * self.core + h, 4) for x in self.X] for h in self.H]
        self.row = 128 * self.U[0][0] + 32 * self.y + 16 * self.odd[0]
        self.relay = jnp.logical_or(self.U[0][0] < 3, jnp.logical_and(self.y == 0, self.odd[0] == 0))
        self.ds = [self.s, self.core, 2 - 2 * self.zl + self.core, 2 + self.core]
        self.dk = [0, 1 - self.zl, 1, self.zl]

    def greet(self):
        barrier = pltpu.get_barrier_semaphore()

        def hello(bucket, span):
            pl.semaphore_signal(barrier, inc=1, device_id=(bucket, span), device_id_type=MESH)

        beyond = rem8_pair(self)
        for dx, dy, d in FAR_FIRST:
            part = 16 * self.X[dx] + 4 * self.Y[dy]
            if dx or dy or d:
                hello(part + self.hz[d], self.hs[d])
            if d == 2:
                hello(part + beyond, self.s)
        for o in (self.buddy, self.cross, self.diag):
            hello(self.me, o)
        hello(16 * self.x + 4 * self.y + self.Z[2], self.s)
        return barrier


GREETED = 63 + 16 + 3 + 1


def rem8_pair(pc):
    return lax.rem(pc.z + 1 + 2 * pc.zl, 4)


STEPS = (0, 1, 2, 1)
FAR_FIRST = sorted(
    ((dx, dy, d) for dx in range(4) for dy in range(4) for d in range(4)),
    key=lambda o: -(STEPS[o[0]] + STEPS[o[1]] + o[2]),
)


def tile_at(ref, row, lane):
    return ref.at[pl.ds(pl.multiple_of(row, 16), 16), pl.ds(pl.multiple_of(lane, 128), 128)]


def wait_tiles(buf, n, ssem, rsem, pc, send):
    ref = buf.at[pl.ds(0, n)]
    d = pltpu.make_async_remote_copy(
        src_ref=ref, dst_ref=ref, send_sem=ssem, recv_sem=rsem, device_id=(pc.me, pc.buddy), device_id_type=MESH
    )
    if send:
        d.wait_send()
    else:
        d.wait_recv()


def leg_one(pc, src, recv, sem_loc, ssem, rsem, columns=(0, 1)):
    for dx, dy, d in FAR_FIRST:
        if not (dx or dy or d) or d // 2 not in columns:
            continue
        u = pc.U[d][dx]

        @pl.when(jnp.logical_or(u < 3, jnp.logical_and(pc.Y[dy] == 0, pc.odd[d] == 0)))
        def _():
            pltpu.make_async_remote_copy(
                src_ref=tile_at(src, 128 * u + 32 * pc.Y[dy] + 16 * pc.odd[d], 128 * (d // 2)),
                dst_ref=recv.at[pc.me], send_sem=ssem, recv_sem=rsem,
                device_id=(16 * pc.X[dx] + 4 * pc.Y[dy] + pc.hz[d], pc.hs[d]), device_id_type=MESH,
            ).start()

    if 0 in columns:
        @pl.when(pc.relay)
        def _():
            pltpu.make_async_copy(tile_at(src, pc.row, 0), recv.at[pc.me], sem_loc).start()


def leg_one_wait(pc, src, recv, sem_loc, ssem, rsem):
    @pl.when(pc.relay)
    def _():
        pltpu.make_async_copy(tile_at(src, pc.row, 0), recv.at[pc.me], sem_loc).wait()
        wait_tiles(recv, 63, ssem, rsem, pc, False)


def leg_two(pc, recv, pick, send, dst, sem_loc, ssem, rsem):
    @pl.when(pc.relay)
    def _():
        for i in range(64):
            send[i] = recv[pick(i)]
        for dx, dy, e in FAR_FIRST:
            if dx or dy or e:
                p = 16 * pc.X[dx] + 4 * pc.Y[dy] + pc.Z[e]
                pltpu.make_async_remote_copy(
                    src_ref=send.at[p], dst_ref=tile_at(dst, pc.row, Q * pc.ds[e] + 128 * pc.dk[e]),
                    send_sem=ssem, recv_sem=rsem.at[pc.dk[e]], device_id=(p, pc.ds[e]), device_id_type=MESH,
                ).start()
        pltpu.make_async_copy(send.at[pc.me], tile_at(dst, pc.row, Q * pc.s), sem_loc).start()


def leg_two_wait(pc, recv, send, dst, sem_loc, ssem, rsem, column):
    if column:
        wait_tiles(recv, TILES // 2, ssem, rsem.at[1], pc, False)
        return

    @pl.when(pc.relay)
    def _():
        pltpu.make_async_copy(send.at[pc.me], tile_at(dst, pc.row, Q * pc.s), sem_loc).wait()
        wait_tiles(recv, TILES // 2 - 1, ssem, rsem.at[0], pc, False)

    @pl.when(jnp.logical_not(pc.relay))
    def _():
        wait_tiles(recv, TILES // 2, ssem, rsem.at[0], pc, False)


def legs_sent(pc, recv, s1, s2, r1):
    @pl.when(pc.relay)
    def _():
        wait_tiles(recv, TILES - 1, s1, r1, pc, True)
        wait_tiles(recv, 63, s2, r1, pc, True)

    @pl.when(jnp.logical_not(pc.relay))
    def _():
        wait_tiles(recv, TILES, s1, r1, pc, True)


def lanes(q, n=Q):
    return pl.ds(pl.multiple_of(q * Q, Q), n)


def dot(a, b, ca=1, cb=0):
    return lax.dot_general(a, b, (((ca,), (cb,)), ((), ())), preferred_element_type=F32)


def quarter_rows(q):
    return pl.ds(pl.multiple_of(q * Q, Q), Q)


def chunk_at(c):
    return pl.ds(c * CHUNK if isinstance(c, int) else pl.multiple_of(c * CHUNK, CHUNK), CHUNK)


def alive_index(index, c, first, lim):
    slots = first + c * CHUNK + lax.broadcasted_iota(jnp.int32, (1, CHUNK), 1)
    return jnp.where(slots < lim[0], index, -1)


def group_column(core, g, z):
    t = lax.rem(g - z + 4, 4)
    upper = jnp.logical_and(t > 0, t < 3).astype(jnp.int32)
    second = (t > 1).astype(jnp.int32)
    return 4 * upper + 2 * core + second


def place_of_row(row, z):
    return 128 * group_column(row // 512, (row // 128) % 4, z) + row % 128


def round_kernel(
    src, tgt, rel_in, sidx_in, tidx_in, kidx_in, planrow_in, lim, plan_in, state_in,
    o_new, o_tgt, o_rel,
    rel, sidx, tidx, kidx, planrow, plan, state, o_src,
    raw, src_raw, low, table, heads, tails, kinds, query, head, tail, relrow, coef, gtail, ghead, grel, tg, sg,
    send1, recv1, send2, quarter, recv3, send4,
    t1, t2send, t2, half, halfin, halfx, rg, r1buf, r2buf, r2send, rax, invcol, inv,
    sem_in, sem_loc, s1, r1, s2, r2, s3, r3, s4, r4, sag, rag, sbk, rbk, st, rt, srel, rrel,
):
    pc = Place()
    cin = []
    for k in range(2):
        g = lax.rem(pc.z + pc.zl + 3 * k - 2 * k * pc.zl, 4)
        at = pl.ds(pl.multiple_of(512 * pc.core + 128 * g, 128), 128)
        cin.append(pltpu.make_async_copy(tgt.at[:, at], raw.at[:, pl.ds(128 * k, 128)], sem_in.at[3 + k]))
    small = [
        pltpu.make_async_copy(a, b, sem_in.at[5 + i]) for i, (a, b) in enumerate((
            (rel_in, rel), (sidx_in, sidx), (tidx_in, tidx), (kidx_in, kidx), (planrow_in, planrow), (plan_in, plan), (state_in, state),
        ))
    ]
    csrc = pltpu.make_async_copy(src, src_raw, sem_in.at[1])
    for c in (*cin, csrc):
        c.start()
    barrier = pc.greet()
    for c in small:
        c.start()
    for c in cin:
        c.wait()
    send1[...] = raw[...].astype(BF)
    pl.semaphore_wait(barrier, GREETED)
    leg_one(pc, send1, recv1, sem_loc.at[0], s1, r1)

    first = pc.s * EDGES
    for c in small:
        c.wait()
    r = rel[...]
    hi = r.astype(BF)
    mid = (r - hi.astype(F32)).astype(BF)
    lo = (r - hi.astype(F32) - mid.astype(F32)).astype(BF)
    rel3 = jnp.concatenate([hi, mid, lo], axis=0)
    here = lax.broadcasted_iota(jnp.int32, (64, 64), 0) == planrow[...]
    found = jnp.sum(jnp.where(here, lax.broadcasted_iota(jnp.int32, (64, 64), 1), 0), axis=1, keepdims=True)
    invcol[...] = jnp.broadcast_to(jnp.minimum(found, 63), (64, 128))
    cinv = pltpu.make_async_copy(invcol, inv, sem_in.at[2])
    cinv.start()
    csrc.wait()
    low[...] = src_raw[...].astype(BF)

    def gather_heads(c, carry):
        at = chunk_at(c)
        rows = lax.broadcasted_iota(jnp.int32, (ROWS, CHUNK), 0)
        hot = (rows == alive_index(sidx[:, at], c, first, lim)).astype(F32).astype(BF)
        heads[:, at] = hot
        h = dot(low[...], hot)
        head[:, at] = h.astype(BF)
        k16 = lax.broadcasted_iota(jnp.int32, (REL, CHUNK), 0)
        khot = (k16 == alive_index(kidx[:, at], c, first, lim)).astype(F32).astype(BF)
        kinds[:, at] = khot
        rr = dot(rel3, jnp.concatenate([khot, khot, khot], axis=0), 0, 0)
        relrow[:, at] = rr
        hr, hm, kr, km = h[:HALF], h[HALF:], rr[:HALF], rr[HALF:]
        query[:, at] = jnp.concatenate([hr * kr - hm * km, hr * km + hm * kr], axis=0).astype(BF)
        return carry

    lax.fori_loop(0, EDGES // CHUNK, gather_heads, 0)
    cinv.wait()
    leg_one_wait(pc, send1, recv1, sem_loc.at[0], s1, r1)
    leg_two(pc, recv1, lambda i: plan[i], send2, table, sem_loc.at[1], s2, r2)

    def mark_tails(c, carry):
        rows = lax.broadcasted_iota(jnp.int32, (ROWS, CHUNK), 0)
        tails[:, chunk_at(c)] = (rows == alive_index(place_of_row(tidx[:, chunk_at(c)], pc.z), c, first, lim)).astype(F32).astype(BF)
        return carry

    lax.fori_loop(0, EDGES // CHUNK, mark_tails, 0)
    def cp(out, q, c, o, i, ss, rs):
        k, row, rows = PIECES[c]
        ref = out.at[pl.ds(row, rows), pl.ds(pl.multiple_of(q * Q + 128 * k, 128), 128)]
        return pltpu.make_async_remote_copy(
            src_ref=ref, dst_ref=ref, send_sem=ss.at[i, c], recv_sem=rs.at[i, c],
            device_id=(pc.me, o), device_id_type=MESH,
        )

    def spread(out, ss, rs):
        across = [cp(out, pc.s, c, pc.cross, 0, ss, rs) for c in range(CH)]
        beside = [cp(out, pc.s, c, pc.buddy, 1, ss, rs) for c in range(CH)]
        passed = [cp(out, pc.cross, c, pc.buddy, 2, ss, rs) for c in range(CH)]
        return across, beside, passed

    across, beside, passed = spread(table, sag, rag)
    for k in range(2):
        leg_two_wait(pc, recv1, send2, table, sem_loc.at[1], s2, r2, k)
        for c in range(2 * k, 2 * k + 2):
            across[c].start()
            beside[c].start()
    for c in range(CH):
        beside[c].wait_recv()
    near = pl.ds(pl.multiple_of(pc.zl * 512, 512), 512)
    far = pl.ds(pl.multiple_of(512 - pc.zl * 512, 512), 512)


    def tails_near(c, carry):
        tail[:, chunk_at(c)] = dot(table[:, near], tails[near, chunk_at(c)]).astype(BF)
        return carry

    for c in range(EDGES // CHUNK):
        tails_near(c, 0)
    for c in range(CH):
        across[c].wait_recv()
        passed[c].start()
    for c in range(CH):
        passed[c].wait_recv()

    def tails_far(c, carry):
        at = chunk_at(c)
        tail[:, at] = (tail[:, at].astype(F32) + dot(table[:, far], tails[far, at])).astype(BF)
        return carry

    for c in range(EDGES // CHUNK):
        tails_far(c, 0)

    def score_span(k, carry):
        base = pl.multiple_of(k * E_CH, 128)
        at = pl.ds(base, E_CH)
        for b in range(E_CH // 128):
            score = dot(query[:, pl.ds(pl.multiple_of(base + 128 * b, 128), 128)], tail[:, at], 0, 0)
            for j in range(E_CH // 128):
                bend = jnp.tanh(0.5 * score[:, 128 * j:128 * j + 128])
                w = (0.5 * NEG_WEIGHT) * bend + 0.5 * NEG_WEIGHT
                if j == b:
                    one = lax.broadcasted_iota(jnp.int32, (128, 128), 0) == lax.broadcasted_iota(jnp.int32, (128, 128), 1)
                    w = jnp.where(one, 0.5 * bend - 0.5, w)
                coef[k, pl.ds(128 * b, 128), pl.ds(128 * j, 128)] = w.astype(BF)
        gtail[:, at] = dot(query[:, at], coef[k]).astype(BF)
        return carry

    lax.fori_loop(0, SPANS, score_span, 0)

    def rc(src_ref, dst_ref, i, o):
        return pltpu.make_async_remote_copy(
            src_ref=src_ref, dst_ref=dst_ref, send_sem=st.at[i], recv_sem=rt.at[i], device_id=(pc.me, o), device_id_type=MESH
        )

    def to_bucket(src_ref, dst_ref, i, p):
        return pltpu.make_async_remote_copy(
            src_ref=src_ref, dst_ref=dst_ref, send_sem=srel.at[i], recv_sem=rrel.at[i], device_id=(p, pc.s), device_id_type=MESH
        )

    def target_sum(part):
        tg[:, part] = dot(gtail[...], tails[part, :], 1, 1).astype(BF)

    ta = rc(tg.at[:, lanes(pc.diag)], t1.at[1], 0, pc.buddy)
    tb = rc(tg.at[:, lanes(pc.buddy)], t1.at[0], 1, pc.buddy)
    tc = [rc(t2send.at[:, pl.ds(128 * k, 128)], t2.at[:, pl.ds(128 * k, 128)], 5 + 9 * k, pc.cross) for k in range(2)]
    target_sum(far)
    ta.start()
    target_sum(near)
    tb.start()
    ta.wait_recv()
    t2send[...] = (tg[:, lanes(pc.cross)].astype(F32) + t1[1].astype(F32)).astype(BF)
    tc[1].start()
    tc[0].start()
    def query_span(k, carry):
        at = pl.ds(pl.multiple_of(k * E_CH, 128), E_CH)
        gq = dot(tail[:, at], coef[k], 1, 1)
        gr, gm = gq[:HALF], gq[HALF:]
        rr = relrow[:, at]
        kr, km = rr[:HALF], rr[HALF:]
        h = head[:, at].astype(F32)
        hr, hm = h[:HALF], h[HALF:]
        ghead[:, at] = jnp.concatenate([gr * kr + gm * km, gm * kr - gr * km], axis=0).astype(BF)
        grel[:, at] = jnp.concatenate([gr * hr + gm * hm, gm * hr - gr * hm], axis=0).astype(BF)
        return carry

    def quarter_column(k):
        tc[k].wait_recv()
        at = pl.ds(pl.multiple_of(pc.s * Q + 128 * k, 128), 128)
        col = pl.ds(128 * k, 128)
        quarter[:, col] = (tg[:, at].astype(F32) + t1[0, :, col].astype(F32) + t2[:, col].astype(F32)).astype(BF)
        leg_one(pc, quarter, recv3, sem_loc.at[2], s3, r3, (k,))

    lax.fori_loop(0, SPANS, query_span, 0)

    def source_sum(part):
        sg[:, part] = dot(ghead[...], heads[part, :], 1, 1).astype(BF)

    sa = rc(sg.at[:, lanes(pc.buddy)], halfin.at[0], 2, pc.buddy)
    sb = rc(sg.at[:, lanes(pc.diag)], halfin.at[1], 3, pc.buddy)
    ra = rc(rg, r1buf, 4, pc.buddy)
    rb = rc(r2send, r2buf, 6, pc.cross)
    sc = rc(half.at[0], halfx.at[1], 7, pc.cross)
    sd = [rc(half.at[1, pl.ds(a, n)], halfx.at[0, pl.ds(a, n)], i, pc.cross) for i, a, n in ((8, 0, 208), (15, 208, 192))]
    source_sum(near)
    sa.start()
    tb.wait_recv()
    quarter_column(1)
    rg[:, 0:D] = dot(kinds[...], grel[...], 1, 1)
    rg[:, D:512] = jnp.zeros((REL, 512 - D), F32)
    ra.start()
    quarter_column(0)
    ra.wait_recv()
    r2send[...] = rg[...] + r1buf[...]
    rb.start()
    sa.wait_recv()
    half[0] = (sg[:, lanes(pc.s)].astype(F32) + halfin[0].astype(F32)).astype(BF)
    sc.start()
    source_sum(far)
    sb.start()

    col = pl.ds(pl.multiple_of(pc.s * 128, 128), 128)
    px = [16 * x + 4 * pc.y + pc.z for x in pc.X[1:]]
    py = [16 * pc.x + 4 * y + pc.z for y in pc.Y[1:]]
    pz = [16 * pc.x + 4 * pc.y + z for z in pc.Z[1:]]

    def axis(i, coord, peers, total):
        rax[i, coord] = total
        for p in peers:
            to_bucket(rax.at[i, coord], rax.at[i, coord], i, p).start()

    def axis_wait(i, send=False):
        ref = rax.at[i, pl.ds(0, 3)]
        d = to_bucket(ref, ref, i, px[0])
        if send:
            d.wait_send()
            return None
        d.wait_recv()
        return (rax[i, 0] + rax[i, 1]) + (rax[i, 2] + rax[i, 3])

    sb.wait_recv()
    half[1] = (sg[:, lanes(pc.cross)].astype(F32) + halfin[1].astype(F32)).astype(BF)
    sd[0].start()
    rb.wait_recv()
    axis(0, pc.x, px, r2send[:, col] + r2buf[:, col])
    leg_one_wait(pc, quarter, recv3, sem_loc.at[2], s3, r3)
    leg_two(pc, recv3, lambda i: inv[i, 0], send4, o_tgt, sem_loc.at[3], s4, r4)
    sd[1].start()
    axis(1, pc.y, py, axis_wait(0))
    axis(2, pc.z, pz, axis_wait(1))
    across2, beside2, passed2 = spread(o_tgt, sbk, rbk)
    for k in range(2):
        leg_two_wait(pc, recv3, send4, o_tgt, sem_loc.at[3], s4, r4, k)
        for c in range(2 * k, 2 * k + 2):
            across2[c].start()
            beside2[c].start()
    sc.wait_recv()
    sd[0].wait_recv()
    sd[1].wait_recv()
    def source_step(q):
        at = lanes(q)
        grad = o_src[:, at].astype(F32)
        total = state[:, at] + jnp.sum(grad * grad, axis=0, keepdims=True) * (1.0 / D)
        o_new[:, at] = src_raw[:, at] - grad * (LEARN_RATE / jnp.sqrt(total))

    o_src[:, lanes(pc.s)] = (half[0].astype(F32) + halfx[0].astype(F32)).astype(BF)
    o_src[:, lanes(pc.cross)] = (half[1].astype(F32) + halfx[1].astype(F32)).astype(BF)
    se = rc(o_src.at[:, lanes(pc.s)], o_src.at[:, lanes(pc.s)], 9, pc.buddy)
    sf = rc(o_src.at[:, lanes(pc.cross)], o_src.at[:, lanes(pc.cross)], 10, pc.buddy)
    se.start()
    sf.start()
    source_step(pc.s)
    source_step(pc.cross)
    for c in range(CH):
        if c == CH // 2:
            o_rel[:, col] = axis_wait(2)
            rel_out = [rc(o_rel.at[:, col], o_rel.at[:, col], 11 + i, o) for i, o in enumerate((pc.buddy, pc.cross, pc.diag))]
            for r in rel_out:
                r.start()
        across2[c].wait_recv()
        passed2[c].start()
    se.wait_recv()
    sf.wait_recv()
    source_step(pc.buddy)
    source_step(pc.diag)
    for c in range(CH):
        beside2[c].wait_recv()
        passed2[c].wait_recv()
    for c in rel_out:
        c.wait_recv()

    for c in (ta, tb, *tc, sa, sb, sc, *sd, se, sf, ra, rb, *rel_out, *across, *beside, *passed, *across2, *beside2, *passed2):
        c.wait_send()
    for i in range(3):
        axis_wait(i, True)
    legs_sent(pc, recv1, s1, s2, r1)
    legs_sent(pc, recv3, s3, s4, r3)


def training_round(source_t, target_t, relation, sidx, tidx, kidx, counts, plan, state):
    vm = pl.BlockSpec(memory_space=pltpu.VMEM)
    hb = pl.BlockSpec(memory_space=pltpu.HBM)
    dma = pltpu.SemaphoreType.DMA

    def i32(*shape):
        return pltpu.VMEM(shape, jnp.int32)

    def bf(*shape):
        return pltpu.VMEM(shape, BF)

    def f(*shape):
        return pltpu.VMEM(shape, F32)

    tiles = bf(64, 16, 128)
    kept = [
        pltpu.with_memory_space_constraint(a, pltpu.HBM) for a in (source_t, target_t, relation, sidx, tidx, kidx, plan[None, :], plan, state)
    ]
    return pl.pallas_call(
        round_kernel,
        out_shape=(
            jax.ShapeDtypeStruct((D, ROWS), F32), jax.ShapeDtypeStruct((D, ROWS), BF), jax.ShapeDtypeStruct((REL, 512), F32),
        ),
        in_specs=[hb] * 7 + [pl.BlockSpec(memory_space=pltpu.SMEM)] + [hb] * 2,
        out_specs=(vm, vm, vm),
        scratch_shapes=[
            f(REL, D), i32(1, EDGES), i32(1, EDGES), i32(1, EDGES), i32(1, 64), pltpu.SMEM((64,), jnp.int32), f(1, ROWS), bf(D, ROWS),
            f(D, Q), f(D, ROWS), bf(D, ROWS), bf(D, ROWS), bf(ROWS, EDGES), bf(ROWS, EDGES), bf(REL, EDGES),
            bf(D, EDGES), bf(D, EDGES), bf(D, EDGES), f(D, EDGES), bf(SPANS, E_CH, E_CH),
            bf(D, EDGES), bf(D, EDGES), bf(D, EDGES), bf(D, ROWS), bf(D, ROWS),
            bf(D, Q), tiles, tiles, bf(D, Q), tiles, tiles,
            bf(2, D, Q), bf(D, Q), bf(D, Q), bf(2, D, Q), bf(2, D, Q), bf(2, D, Q),
            f(REL, 512), f(REL, 512), f(REL, 512), f(REL, 512), f(3, 4, REL, 128),
            pltpu.VMEM((64, 128), jnp.int32), pltpu.SMEM((64, 128), jnp.int32),
            dma((13,)), dma((4,)), dma, dma, dma, dma((2,)), dma, dma, dma, dma((2,)),
            dma((3, CH)), dma((3, CH)), dma((3, CH)), dma((3, CH)), dma((16,)), dma((16,)), dma((3,)), dma((3,)),
        ],
        compiler_params=pltpu.CompilerParams(collective_id=0, has_side_effects=True, vmem_limit_bytes=46 << 20),
        name="training_round",
    )(*kept[:7], counts, *kept[7:])


def adagrad_kernel(new, wt, st, gt, wr, sr, gr, o_s, o_t, o_r, buf, sem):
    copies = []
    for q in range(ROWS // Q):
        at = pl.ds(q * 96 if q else 0, 96 if q < 3 else 112)
        copies.append(pltpu.make_async_copy(new.at[at, :], o_s.at[at, :], sem.at[ROWS // Q + q]))
        copies[-1].start()
    z = lax.rem(lax.axis_index("bucket"), 4)
    for q in range(ROWS // Q):
        at = pl.ds(q * Q, Q)
        cols = [pl.multiple_of(128 * group_column(q // 2, 2 * (q % 2) + h, z), 128) for h in range(2)]
        grad = jnp.concatenate([gt[:, pl.ds(c, 128)] for c in cols], axis=1).astype(F32)
        total = st[:, at] + jnp.sum(grad * grad, axis=0, keepdims=True) * (1.0 / D)
        buf[q] = wt[:, at] - grad * (LEARN_RATE / jnp.sqrt(total))
        copies.append(pltpu.make_async_copy(buf.at[q], o_t.at[:, at], sem.at[q]))
        copies[-1].start()
    grad = gr[:, 0:D]
    same = lax.broadcasted_iota(jnp.int32, (REL, REL), 0) == lax.broadcasted_iota(jnp.int32, (REL, REL), 1)
    state = jnp.sum(jnp.where(same, sr[...], 0.0), axis=1, keepdims=True)
    total = state + jnp.sum(grad * grad, axis=1, keepdims=True) * (1.0 / D)
    o_r[...] = wr[...] - grad * (LEARN_RATE / jnp.sqrt(total))
    for c in copies:
        c.wait()


def adagrad(*args):
    vm = pl.BlockSpec(memory_space=pltpu.VMEM)
    hb = pl.BlockSpec(memory_space=pl.ANY)
    return pl.pallas_call(
        adagrad_kernel,
        out_shape=(
            jax.ShapeDtypeStruct((D, ROWS), F32), jax.ShapeDtypeStruct((D, ROWS), F32), jax.ShapeDtypeStruct((REL, D), F32),
        ),
        in_specs=[vm] * 7,
        out_specs=(hb, hb, vm),
        scratch_shapes=[pltpu.VMEM((ROWS // Q, D, Q), F32), pltpu.SemaphoreType.DMA((2 * ROWS // Q,))],
        compiler_params=pltpu.CompilerParams(vmem_limit_bytes=24 << 20),
        name="adagrad",
    )(*args)


def per_device(source_table, target_table, source_state, target_state, relation, relation_state,
               plan, source_index, target_index, relation_index, edge_counts):
    source_t, target_t = source_table.T, target_table.T
    new, tg, rg = training_round(
        source_t, target_t, relation, source_index, target_index, relation_index, edge_counts, plan, source_state[None, :]
    )
    ns, nt, nr = adagrad(new, target_t, target_state[None, :], tg, relation, relation_state[None, :], rg)
    return ns.T, nt.T, nr


def solution(mesh):
    placed = (
        P("bucket", None), P("bucket", None), P("bucket"), P("bucket"), P(), P(), P(),
        P("bucket", "span"), P("bucket", "span"), P("bucket", "span"), P("bucket"),
    )
    return jax.shard_map(
        per_device,
        mesh=mesh,
        in_specs=placed,
        out_specs=(P("bucket", None), P("bucket", None), P()),
        check_vma=False,
    )
```

```python
import functools

import jax
import jax.numpy as jnp
from jax import lax
from jax.experimental import pallas as pl
from jax.experimental.pallas import tpu as pltpu
from jax.sharding import PartitionSpec as P

MESH = pl.DeviceIdType.MESH
BF = jnp.bfloat16
F32 = jnp.float32
E_CH = 640
LEARN_RATE = 0.25
NEG_WEIGHT = 0.03125
D = 400
HALF = 200
ROWS = 1024
Q = 256
EDGES = 2560
SPANS = 4
REL = 16
TILES = 50
PIECES = ((0, 0, 208), (0, 208, 192), (1, 0, 208), (1, 208, 192))
CH = len(PIECES)
CHUNK = 512


class Place:
    def __init__(self):
        rem, div = lax.rem, lax.div
        self.me = lax.axis_index("bucket")
        self.s = lax.axis_index("span")
        self.x = div(self.me, 16)
        self.y = rem(div(self.me, 4), 4)
        self.z = rem(self.me, 4)
        self.zl = div(self.s, 2)
        self.core = rem(self.s, 2)
        self.buddy = self.s + 1 - 2 * self.core
        self.cross = rem(self.s + 2, 4)
        self.diag = rem(self.buddy + 2, 4)
        self.X = [rem(self.x + d, 4) for d in range(4)]
        self.Y = [rem(self.y + d, 4) for d in range(4)]
        self.Z = [rem(self.z + d, 4) for d in range(4)]
        way = 2 * self.zl - 1
        height = 2 * self.z + self.zl
        self.H = [rem(height + way * d + 8, 8) for d in range(4)]
        self.hz = [div(h, 2) for h in self.H]
        self.hs = [2 * rem(h, 2) + self.core for h in self.H]
        self.odd = [rem(d + 1 + self.zl, 2) for d in range(4)]
        self.U = [[rem(x + 2 * self.core + h, 4) for x in self.X] for h in self.H]
        self.row = 128 * self.U[0][0] + 32 * self.y + 16 * self.odd[0]
        self.relay = jnp.logical_or(self.U[0][0] < 3, jnp.logical_and(self.y == 0, self.odd[0] == 0))
        self.ds = [self.s, self.core, 2 - 2 * self.zl + self.core, 2 + self.core]
        self.dk = [0, 1 - self.zl, 1, self.zl]

    def greet(self):
        barrier = pltpu.get_barrier_semaphore()

        def hello(bucket, span):
            pl.semaphore_signal(barrier, inc=1, device_id=(bucket, span), device_id_type=MESH)

        beyond = rem8_pair(self)
        for dx, dy, d in FAR_FIRST:
            part = 16 * self.X[dx] + 4 * self.Y[dy]
            if dx or dy or d:
                hello(part + self.hz[d], self.hs[d])
            if d == 2:
                hello(part + beyond, self.s)
        for o in (self.buddy, self.cross, self.diag):
            hello(self.me, o)
        hello(16 * self.x + 4 * self.y + self.Z[2], self.s)
        return barrier


GREETED = 63 + 16 + 3 + 1


def rem8_pair(pc):
    return lax.rem(pc.z + 1 + 2 * pc.zl, 4)


STEPS = (0, 1, 2, 1)
FAR_FIRST = sorted(
    ((dx, dy, d) for dx in range(4) for dy in range(4) for d in range(4)),
    key=lambda o: -(STEPS[o[0]] + STEPS[o[1]] + o[2]),
)


def tile_at(ref, row, lane):
    return ref.at[pl.ds(pl.multiple_of(row, 16), 16), pl.ds(pl.multiple_of(lane, 128), 128)]


def wait_tiles(buf, n, ssem, rsem, pc, send):
    ref = buf.at[pl.ds(0, n)]
    d = pltpu.make_async_remote_copy(
        src_ref=ref, dst_ref=ref, send_sem=ssem, recv_sem=rsem, device_id=(pc.me, pc.buddy), device_id_type=MESH
    )
    if send:
        d.wait_send()
    else:
        d.wait_recv()


def leg_one(pc, src, recv, sem_loc, ssem, rsem, columns=(0, 1)):
    for dx, dy, d in FAR_FIRST:
        if not (dx or dy or d) or d // 2 not in columns:
            continue
        u = pc.U[d][dx]

        @pl.when(jnp.logical_or(u < 3, jnp.logical_and(pc.Y[dy] == 0, pc.odd[d] == 0)))
        def _():
            pltpu.make_async_remote_copy(
                src_ref=tile_at(src, 128 * u + 32 * pc.Y[dy] + 16 * pc.odd[d], 128 * (d // 2)),
                dst_ref=recv.at[pc.me], send_sem=ssem, recv_sem=rsem,
                device_id=(16 * pc.X[dx] + 4 * pc.Y[dy] + pc.hz[d], pc.hs[d]), device_id_type=MESH,
            ).start()

    if 0 in columns:
        @pl.when(pc.relay)
        def _():
            pltpu.make_async_copy(tile_at(src, pc.row, 0), recv.at[pc.me], sem_loc).start()


def leg_one_wait(pc, src, recv, sem_loc, ssem, rsem):
    @pl.when(pc.relay)
    def _():
        pltpu.make_async_copy(tile_at(src, pc.row, 0), recv.at[pc.me], sem_loc).wait()
        wait_tiles(recv, 63, ssem, rsem, pc, False)


def leg_two(pc, recv, pick, send, dst, sem_loc, ssem, rsem):
    @pl.when(pc.relay)
    def _():
        for i in range(64):
            send[i] = recv[pick(i)]
        for dx, dy, e in FAR_FIRST:
            if dx or dy or e:
                p = 16 * pc.X[dx] + 4 * pc.Y[dy] + pc.Z[e]
                pltpu.make_async_remote_copy(
                    src_ref=send.at[p], dst_ref=tile_at(dst, pc.row, Q * pc.ds[e] + 128 * pc.dk[e]),
                    send_sem=ssem, recv_sem=rsem.at[pc.dk[e]], device_id=(p, pc.ds[e]), device_id_type=MESH,
                ).start()
        pltpu.make_async_copy(send.at[pc.me], tile_at(dst, pc.row, Q * pc.s), sem_loc).start()


def leg_two_wait(pc, recv, send, dst, sem_loc, ssem, rsem, column):
    if column:
        wait_tiles(recv, TILES // 2, ssem, rsem.at[1], pc, False)
        return

    @pl.when(pc.relay)
    def _():
        pltpu.make_async_copy(send.at[pc.me], tile_at(dst, pc.row, Q * pc.s), sem_loc).wait()
        wait_tiles(recv, TILES // 2 - 1, ssem, rsem.at[0], pc, False)

    @pl.when(jnp.logical_not(pc.relay))
    def _():
        wait_tiles(recv, TILES // 2, ssem, rsem.at[0], pc, False)


def legs_sent(pc, recv, s1, s2, r1):
    @pl.when(pc.relay)
    def _():
        wait_tiles(recv, TILES - 1, s1, r1, pc, True)
        wait_tiles(recv, 63, s2, r1, pc, True)

    @pl.when(jnp.logical_not(pc.relay))
    def _():
        wait_tiles(recv, TILES, s1, r1, pc, True)


def lanes(q, n=Q):
    return pl.ds(pl.multiple_of(q * Q, Q), n)


def dot(a, b, ca=1, cb=0):
    return lax.dot_general(a, b, (((ca,), (cb,)), ((), ())), preferred_element_type=F32)


def quarter_rows(q):
    return pl.ds(pl.multiple_of(q * Q, Q), Q)


def chunk_at(c):
    return pl.ds(c * CHUNK if isinstance(c, int) else pl.multiple_of(c * CHUNK, CHUNK), CHUNK)


def alive_index(index, c, first, lim):
    slots = first + c * CHUNK + lax.broadcasted_iota(jnp.int32, (1, CHUNK), 1)
    return jnp.where(slots < lim[0], index, -1)


def group_column(core, g, z):
    t = lax.rem(g - z + 4, 4)
    upper = jnp.logical_and(t > 0, t < 3).astype(jnp.int32)
    second = (t > 1).astype(jnp.int32)
    return 4 * upper + 2 * core + second


def place_of_row(row, z):
    return 128 * group_column(row // 512, (row // 128) % 4, z) + row % 128


def round_kernel(
    src, tgt, rel_in, sidx_in, tidx_in, kidx_in, planrow_in, lim, plan_in, state_in,
    o_new, o_tgt, o_rel,
    rel, sidx, tidx, kidx, planrow, plan, state, o_src,
    raw, src_raw, low, table, heads, tails, kinds, query, head, tail, relrow, coef, gtail, ghead, grel, tg, sg,
    send1, recv1, send2, quarter, recv3, send4,
    t1, t2send, t2, half, halfin, halfx, rg, r1buf, r2buf, r2send, rax, invcol, inv,
    sem_in, sem_loc, s1, r1, s2, r2, s3, r3, s4, r4, sag, rag, sbk, rbk, st, rt, srel, rrel,
):
    pc = Place()
    cin = []
    for k in range(2):
        g = lax.rem(pc.z + pc.zl + 3 * k - 2 * k * pc.zl, 4)
        at = pl.ds(pl.multiple_of(512 * pc.core + 128 * g, 128), 128)
        cin.append(pltpu.make_async_copy(tgt.at[:, at], raw.at[:, pl.ds(128 * k, 128)], sem_in.at[3 + k]))
    small = [
        pltpu.make_async_copy(a, b, sem_in.at[5 + i]) for i, (a, b) in enumerate((
            (rel_in, rel), (sidx_in, sidx), (tidx_in, tidx), (kidx_in, kidx), (planrow_in, planrow), (plan_in, plan), (state_in, state),
        ))
    ]
    csrc = pltpu.make_async_copy(src, src_raw, sem_in.at[1])
    for c in (*cin, csrc):
        c.start()
    barrier = pc.greet()
    for c in small:
        c.start()
    for c in cin:
        c.wait()
    send1[...] = raw[...].astype(BF)
    pl.semaphore_wait(barrier, GREETED)
    leg_one(pc, send1, recv1, sem_loc.at[0], s1, r1)

    first = pc.s * EDGES
    for c in small:
        c.wait()
    r = rel[...]
    hi = r.astype(BF)
    mid = (r - hi.astype(F32)).astype(BF)
    lo = (r - hi.astype(F32) - mid.astype(F32)).astype(BF)
    rel3 = jnp.concatenate([hi, mid, lo], axis=0)
    here = lax.broadcasted_iota(jnp.int32, (64, 64), 0) == planrow[...]
    found = jnp.sum(jnp.where(here, lax.broadcasted_iota(jnp.int32, (64, 64), 1), 0), axis=1, keepdims=True)
    invcol[...] = jnp.broadcast_to(jnp.minimum(found, 63), (64, 128))
    cinv = pltpu.make_async_copy(invcol, inv, sem_in.at[2])
    cinv.start()
    csrc.wait()
    low[...] = src_raw[...].astype(BF)

    def gather_heads(c, carry):
        at = chunk_at(c)
        rows = lax.broadcasted_iota(jnp.int32, (ROWS, CHUNK), 0)
        hot = (rows == alive_index(sidx[:, at], c, first, lim)).astype(F32).astype(BF)
        heads[:, at] = hot
        h = dot(low[...], hot)
        head[:, at] = h.astype(BF)
        k16 = lax.broadcasted_iota(jnp.int32, (REL, CHUNK), 0)
        khot = (k16 == alive_index(kidx[:, at], c, first, lim)).astype(F32).astype(BF)
        kinds[:, at] = khot
        rr = dot(rel3, jnp.concatenate([khot, khot, khot], axis=0), 0, 0)
        relrow[:, at] = rr
        hr, hm, kr, km = h[:HALF], h[HALF:], rr[:HALF], rr[HALF:]
        query[:, at] = jnp.concatenate([hr * kr - hm * km, hr * km + hm * kr], axis=0).astype(BF)
        return carry

    lax.fori_loop(0, EDGES // CHUNK, gather_heads, 0)
    cinv.wait()
    leg_one_wait(pc, send1, recv1, sem_loc.at[0], s1, r1)
    leg_two(pc, recv1, lambda i: plan[i], send2, table, sem_loc.at[1], s2, r2)

    def mark_tails(c, carry):
        rows = lax.broadcasted_iota(jnp.int32, (ROWS, CHUNK), 0)
        tails[:, chunk_at(c)] = (rows == alive_index(place_of_row(tidx[:, chunk_at(c)], pc.z), c, first, lim)).astype(F32).astype(BF)
        return carry

    lax.fori_loop(0, EDGES // CHUNK, mark_tails, 0)
    def cp(out, q, c, o, i, ss, rs):
        k, row, rows = PIECES[c]
        ref = out.at[pl.ds(row, rows), pl.ds(pl.multiple_of(q * Q + 128 * k, 128), 128)]
        return pltpu.make_async_remote_copy(
            src_ref=ref, dst_ref=ref, send_sem=ss.at[i, c], recv_sem=rs.at[i, c],
            device_id=(pc.me, o), device_id_type=MESH,
        )

    def spread(out, ss, rs):
        across = [cp(out, pc.s, c, pc.cross, 0, ss, rs) for c in range(CH)]
        beside = [cp(out, pc.s, c, pc.buddy, 1, ss, rs) for c in range(CH)]
        passed = [cp(out, pc.cross, c, pc.buddy, 2, ss, rs) for c in range(CH)]
        return across, beside, passed

    across, beside, passed = spread(table, sag, rag)
    for k in range(2):
        leg_two_wait(pc, recv1, send2, table, sem_loc.at[1], s2, r2, k)
        for c in range(2 * k, 2 * k + 2):
            across[c].start()
            beside[c].start()
    for c in range(CH):
        beside[c].wait_recv()
    near = pl.ds(pl.multiple_of(pc.zl * 512, 512), 512)
    far = pl.ds(pl.multiple_of(512 - pc.zl * 512, 512), 512)


    def tails_near(c, carry):
        tail[:, chunk_at(c)] = dot(table[:, near], tails[near, chunk_at(c)]).astype(BF)
        return carry

    for c in range(EDGES // CHUNK):
        tails_near(c, 0)
    for c in range(CH):
        across[c].wait_recv()
        passed[c].start()
    for c in range(CH):
        passed[c].wait_recv()

    def tails_far(c, carry):
        at = chunk_at(c)
        tail[:, at] = (tail[:, at].astype(F32) + dot(table[:, far], tails[far, at])).astype(BF)
        return carry

    for c in range(EDGES // CHUNK):
        tails_far(c, 0)

    def score_span(k, carry):
        base = pl.multiple_of(k * E_CH, 128)
        at = pl.ds(base, E_CH)
        for b in range(E_CH // 128):
            score = dot(query[:, pl.ds(pl.multiple_of(base + 128 * b, 128), 128)], tail[:, at], 0, 0)
            for j in range(E_CH // 128):
                bend = jnp.tanh(0.5 * score[:, 128 * j:128 * j + 128])
                w = (0.5 * NEG_WEIGHT) * bend + 0.5 * NEG_WEIGHT
                if j == b:
                    one = lax.broadcasted_iota(jnp.int32, (128, 128), 0) == lax.broadcasted_iota(jnp.int32, (128, 128), 1)
                    w = jnp.where(one, 0.5 * bend - 0.5, w)
                coef[k, pl.ds(128 * b, 128), pl.ds(128 * j, 128)] = w.astype(BF)
        gtail[:, at] = dot(query[:, at], coef[k]).astype(BF)
        return carry

    for k in range(SPANS):
        score_span(k, 0)

    def rc(src_ref, dst_ref, i, o):
        return pltpu.make_async_remote_copy(
            src_ref=src_ref, dst_ref=dst_ref, send_sem=st.at[i], recv_sem=rt.at[i], device_id=(pc.me, o), device_id_type=MESH
        )

    def to_bucket(src_ref, dst_ref, i, p):
        return pltpu.make_async_remote_copy(
            src_ref=src_ref, dst_ref=dst_ref, send_sem=srel.at[i], recv_sem=rrel.at[i], device_id=(p, pc.s), device_id_type=MESH
        )

    def target_sum(part):
        tg[:, part] = dot(gtail[...], tails[part, :], 1, 1).astype(BF)

    ta = rc(tg.at[:, lanes(pc.diag)], t1.at[1], 0, pc.buddy)
    tb = rc(tg.at[:, lanes(pc.buddy)], t1.at[0], 1, pc.buddy)
    tc = [rc(t2send.at[:, pl.ds(128 * k, 128)], t2.at[:, pl.ds(128 * k, 128)], 5 + 9 * k, pc.cross) for k in range(2)]
    target_sum(far)
    ta.start()
    target_sum(near)
    tb.start()
    ta.wait_recv()
    t2send[...] = (tg[:, lanes(pc.cross)].astype(F32) + t1[1].astype(F32)).astype(BF)
    tc[1].start()
    tc[0].start()
    def query_span(k, carry):
        at = pl.ds(pl.multiple_of(k * E_CH, 128), E_CH)
        gq = dot(tail[:, at], coef[k], 1, 1)
        gr, gm = gq[:HALF], gq[HALF:]
        rr = relrow[:, at]
        kr, km = rr[:HALF], rr[HALF:]
        h = head[:, at].astype(F32)
        hr, hm = h[:HALF], h[HALF:]
        ghead[:, at] = jnp.concatenate([gr * kr + gm * km, gm * kr - gr * km], axis=0).astype(BF)
        grel[:, at] = jnp.concatenate([gr * hr + gm * hm, gm * hr - gr * hm], axis=0).astype(BF)
        return carry

    def quarter_column(k):
        tc[k].wait_recv()
        at = pl.ds(pl.multiple_of(pc.s * Q + 128 * k, 128), 128)
        col = pl.ds(128 * k, 128)
        quarter[:, col] = (tg[:, at].astype(F32) + t1[0, :, col].astype(F32) + t2[:, col].astype(F32)).astype(BF)
        leg_one(pc, quarter, recv3, sem_loc.at[2], s3, r3, (k,))

    for k in range(SPANS):
        query_span(k, 0)

    def source_sum(part):
        sg[:, part] = dot(ghead[...], heads[part, :], 1, 1).astype(BF)

    sa = rc(sg.at[:, lanes(pc.buddy)], halfin.at[0], 2, pc.buddy)
    sb = rc(sg.at[:, lanes(pc.diag)], halfin.at[1], 3, pc.buddy)
    ra = rc(rg, r1buf, 4, pc.buddy)
    rb = rc(r2send, r2buf, 6, pc.cross)
    sc = rc(half.at[0], halfx.at[1], 7, pc.cross)
    sd = [rc(half.at[1, pl.ds(a, n)], halfx.at[0, pl.ds(a, n)], i, pc.cross) for i, a, n in ((8, 0, 208), (15, 208, 192))]
    source_sum(near)
    sa.start()
    tb.wait_recv()
    quarter_column(1)
    rg[:, 0:D] = dot(kinds[...], grel[...], 1, 1)
    rg[:, D:512] = jnp.zeros((REL, 512 - D), F32)
    ra.start()
    quarter_column(0)
    ra.wait_recv()
    r2send[...] = rg[...] + r1buf[...]
    rb.start()
    sa.wait_recv()
    half[0] = (sg[:, lanes(pc.s)].astype(F32) + halfin[0].astype(F32)).astype(BF)
    sc.start()
    source_sum(far)
    sb.start()

    col = pl.ds(pl.multiple_of(pc.s * 128, 128), 128)
    px = [16 * x + 4 * pc.y + pc.z for x in pc.X[1:]]
    py = [16 * pc.x + 4 * y + pc.z for y in pc.Y[1:]]
    pz = [16 * pc.x + 4 * pc.y + z for z in pc.Z[1:]]

    def axis(i, coord, peers, total):
        rax[i, coord] = total
        for p in peers:
            to_bucket(rax.at[i, coord], rax.at[i, coord], i, p).start()

    def axis_wait(i, send=False):
        ref = rax.at[i, pl.ds(0, 3)]
        d = to_bucket(ref, ref, i, px[0])
        if send:
            d.wait_send()
            return None
        d.wait_recv()
        return (rax[i, 0] + rax[i, 1]) + (rax[i, 2] + rax[i, 3])

    sb.wait_recv()
    half[1] = (sg[:, lanes(pc.cross)].astype(F32) + halfin[1].astype(F32)).astype(BF)
    sd[0].start()
    rb.wait_recv()
    axis(0, pc.x, px, r2send[:, col] + r2buf[:, col])
    leg_one_wait(pc, quarter, recv3, sem_loc.at[2], s3, r3)
    leg_two(pc, recv3, lambda i: inv[i, 0], send4, o_tgt, sem_loc.at[3], s4, r4)
    sd[1].start()
    axis(1, pc.y, py, axis_wait(0))
    axis(2, pc.z, pz, axis_wait(1))
    across2, beside2, passed2 = spread(o_tgt, sbk, rbk)
    for k in range(2):
        leg_two_wait(pc, recv3, send4, o_tgt, sem_loc.at[3], s4, r4, k)
        for c in range(2 * k, 2 * k + 2):
            across2[c].start()
            beside2[c].start()
    sc.wait_recv()
    sd[0].wait_recv()
    sd[1].wait_recv()
    def source_step(q):
        at = lanes(q)
        grad = o_src[:, at].astype(F32)
        total = state[:, at] + jnp.sum(grad * grad, axis=0, keepdims=True) * (1.0 / D)
        o_new[:, at] = src_raw[:, at] - grad * (LEARN_RATE / jnp.sqrt(total))

    o_src[:, lanes(pc.s)] = (half[0].astype(F32) + halfx[0].astype(F32)).astype(BF)
    o_src[:, lanes(pc.cross)] = (half[1].astype(F32) + halfx[1].astype(F32)).astype(BF)
    se = rc(o_src.at[:, lanes(pc.s)], o_src.at[:, lanes(pc.s)], 9, pc.buddy)
    sf = rc(o_src.at[:, lanes(pc.cross)], o_src.at[:, lanes(pc.cross)], 10, pc.buddy)
    se.start()
    sf.start()
    source_step(pc.s)
    source_step(pc.cross)
    for c in range(CH):
        if c == CH // 2:
            o_rel[:, col] = axis_wait(2)
            rel_out = [rc(o_rel.at[:, col], o_rel.at[:, col], 11 + i, o) for i, o in enumerate((pc.buddy, pc.cross, pc.diag))]
            for r in rel_out:
                r.start()
        across2[c].wait_recv()
        passed2[c].start()
    se.wait_recv()
    sf.wait_recv()
    source_step(pc.buddy)
    source_step(pc.diag)
    for c in range(CH):
        beside2[c].wait_recv()
        passed2[c].wait_recv()
    for c in rel_out:
        c.wait_recv()

    for c in (ta, tb, *tc, sa, sb, sc, *sd, se, sf, ra, rb, *rel_out, *across, *beside, *passed, *across2, *beside2, *passed2):
        c.wait_send()
    for i in range(3):
        axis_wait(i, True)
    legs_sent(pc, recv1, s1, s2, r1)
    legs_sent(pc, recv3, s3, s4, r3)


def training_round(source_t, target_t, relation, sidx, tidx, kidx, counts, plan, state):
    vm = pl.BlockSpec(memory_space=pltpu.VMEM)
    hb = pl.BlockSpec(memory_space=pltpu.HBM)
    dma = pltpu.SemaphoreType.DMA

    def i32(*shape):
        return pltpu.VMEM(shape, jnp.int32)

    def bf(*shape):
        return pltpu.VMEM(shape, BF)

    def f(*shape):
        return pltpu.VMEM(shape, F32)

    tiles = bf(64, 16, 128)
    kept = [
        pltpu.with_memory_space_constraint(a, pltpu.HBM) for a in (source_t, target_t, relation, sidx, tidx, kidx, plan[None, :], plan, state)
    ]
    return pl.pallas_call(
        round_kernel,
        out_shape=(
            jax.ShapeDtypeStruct((D, ROWS), F32), jax.ShapeDtypeStruct((D, ROWS), BF), jax.ShapeDtypeStruct((REL, 512), F32),
        ),
        in_specs=[hb] * 7 + [pl.BlockSpec(memory_space=pltpu.SMEM)] + [hb] * 2,
        out_specs=(vm, vm, vm),
        scratch_shapes=[
            f(REL, D), i32(1, EDGES), i32(1, EDGES), i32(1, EDGES), i32(1, 64), pltpu.SMEM((64,), jnp.int32), f(1, ROWS), bf(D, ROWS),
            f(D, Q), f(D, ROWS), bf(D, ROWS), bf(D, ROWS), bf(ROWS, EDGES), bf(ROWS, EDGES), bf(REL, EDGES),
            bf(D, EDGES), bf(D, EDGES), bf(D, EDGES), f(D, EDGES), bf(SPANS, E_CH, E_CH),
            bf(D, EDGES), bf(D, EDGES), bf(D, EDGES), bf(D, ROWS), bf(D, ROWS),
            bf(D, Q), tiles, tiles, bf(D, Q), tiles, tiles,
            bf(2, D, Q), bf(D, Q), bf(D, Q), bf(2, D, Q), bf(2, D, Q), bf(2, D, Q),
            f(REL, 512), f(REL, 512), f(REL, 512), f(REL, 512), f(3, 4, REL, 128),
            pltpu.VMEM((64, 128), jnp.int32), pltpu.SMEM((64, 128), jnp.int32),
            dma((13,)), dma((4,)), dma, dma, dma, dma((2,)), dma, dma, dma, dma((2,)),
            dma((3, CH)), dma((3, CH)), dma((3, CH)), dma((3, CH)), dma((16,)), dma((16,)), dma((3,)), dma((3,)),
        ],
        compiler_params=pltpu.CompilerParams(collective_id=0, has_side_effects=True, vmem_limit_bytes=46 << 20),
        name="training_round",
    )(*kept[:7], counts, *kept[7:])


def adagrad_kernel(new, wt, st, gt, wr, sr, gr, o_s, o_t, o_r, buf, sem):
    copies = []
    for q in range(ROWS // Q):
        at = pl.ds(q * 96 if q else 0, 96 if q < 3 else 112)
        copies.append(pltpu.make_async_copy(new.at[at, :], o_s.at[at, :], sem.at[ROWS // Q + q]))
        copies[-1].start()
    z = lax.rem(lax.axis_index("bucket"), 4)
    for q in range(ROWS // Q):
        at = pl.ds(q * Q, Q)
        cols = [pl.multiple_of(128 * group_column(q // 2, 2 * (q % 2) + h, z), 128) for h in range(2)]
        grad = jnp.concatenate([gt[:, pl.ds(c, 128)] for c in cols], axis=1).astype(F32)
        total = st[:, at] + jnp.sum(grad * grad, axis=0, keepdims=True) * (1.0 / D)
        buf[q] = wt[:, at] - grad * (LEARN_RATE / jnp.sqrt(total))
        copies.append(pltpu.make_async_copy(buf.at[q], o_t.at[:, at], sem.at[q]))
        copies[-1].start()
    grad = gr[:, 0:D]
    same = lax.broadcasted_iota(jnp.int32, (REL, REL), 0) == lax.broadcasted_iota(jnp.int32, (REL, REL), 1)
    state = jnp.sum(jnp.where(same, sr[...], 0.0), axis=1, keepdims=True)
    total = state + jnp.sum(grad * grad, axis=1, keepdims=True) * (1.0 / D)
    o_r[...] = wr[...] - grad * (LEARN_RATE / jnp.sqrt(total))
    for c in copies:
        c.wait()


def adagrad(*args):
    vm = pl.BlockSpec(memory_space=pltpu.VMEM)
    hb = pl.BlockSpec(memory_space=pl.ANY)
    return pl.pallas_call(
        adagrad_kernel,
        out_shape=(
            jax.ShapeDtypeStruct((D, ROWS), F32), jax.ShapeDtypeStruct((D, ROWS), F32), jax.ShapeDtypeStruct((REL, D), F32),
        ),
        in_specs=[vm] * 7,
        out_specs=(hb, hb, vm),
        scratch_shapes=[pltpu.VMEM((ROWS // Q, D, Q), F32), pltpu.SemaphoreType.DMA((2 * ROWS // Q,))],
        compiler_params=pltpu.CompilerParams(vmem_limit_bytes=24 << 20),
        name="adagrad",
    )(*args)


def per_device(source_table, target_table, source_state, target_state, relation, relation_state,
               plan, source_index, target_index, relation_index, edge_counts):
    source_t, target_t = source_table.T, target_table.T
    new, tg, rg = training_round(
        source_t, target_t, relation, source_index, target_index, relation_index, edge_counts, plan, source_state[None, :]
    )
    ns, nt, nr = adagrad(new, target_t, target_state[None, :], tg, relation, relation_state[None, :], rg)
    return ns.T, nt.T, nr


def solution(mesh):
    placed = (
        P("bucket", None), P("bucket", None), P("bucket"), P("bucket"), P(), P(), P(),
        P("bucket", "span"), P("bucket", "span"), P("bucket", "span"), P("bucket"),
    )
    return jax.shard_map(
        per_device,
        mesh=mesh,
        in_specs=placed,
        out_specs=(P("bucket", None), P("bucket", None), P()),
        check_vma=False,
    )
```
